256 devices in a mesh: ctx: 32 (over y, x, core), head: 8 (over z).
Axes of the slice: x: 4, y: 4, z: 8, core: 2. Of those that a mesh axis runs over, the one named last changes fastest.
Arguments:
- hits_in: bfloat16 [32768, 1024], P(('ctx', 'head')), may hold values from -32 to 32
- w_query: bfloat16 [1024, 512], replicated, may hold values from -0.25 to 0.25
- w_key: bfloat16 [1024, 512], replicated, may hold values from -0.25 to 0.25
- w_value: bfloat16 [1024, 512], replicated, may hold values from -0.1875 to 0.1875
- w_out: bfloat16 [512, 1024], replicated, may hold values from -0.5 to 0.5
- grad_y: bfloat16 [32768, 1024], P(('ctx', 'head')), may hold values from -6 to 6
- block_cell: int32 [256], replicated, may hold values from 0 to 255, each once
- cell_mask: int32 [256, 256], replicated, may hold values from 0 to 1, as said below
Outputs:
- layer_out: bfloat16 [32768, 1024], P(('ctx', 'head'))
- grad_hits: bfloat16 [32768, 1024], P(('ctx', 'head'))
The draws below stay inside these ranges and needn't reach their ends.
Inputs may be any that keep to these rules, and one draw needn't show every extreme that they name: `cell_mask`: entries are 0 or 1; every cell may attend to itself; no row and no column holds more than 21 ones. `block_cell`: each cell is named by exactly one block.
All inputs are finite; a program needn't handle non-finite values.
Results may differ from the reference program's by a relative error of at most 0.03.
The reference program's roundings to bfloat16 on the way count: a program that leaves them out, or rounds other values in their place, can miss the bound.
Values may be sent and summed in bfloat16 or wider, within the bound.
No kernel may reach another device: no remote copies, remote signals or barrier semaphores. Data moves between devices by JAX's collectives and lax.ppermute only.
A program may use at most 192 MiB of HBM per device.

```python
import jax
import jax.numpy as jnp
from jax import lax

HEADS = 8
HEAD_DIM = 64
D = 1024
INNER = 512
BLOCK = 128
PHI_CELLS = 8
KB_MAX = 21
HITS = 32768
NB = 256


def draw_hits_in(key, part):
    base = jax.random.normal(key, (HITS, D), jnp.float32)
    return jnp.clip(base, -4.0, 4.0).astype(jnp.bfloat16)


def draw_cell_mask(key, part):
    index = jnp.arange(NB, dtype=jnp.int32)
    eta = index // PHI_CELLS
    phi = index % PHI_CELLS
    reach = 1 + eta % 3
    pair_reach = jnp.maximum(reach[:, None], reach[None, :])
    eta_gap = jnp.abs(eta[:, None] - eta[None, :])
    phi_gap = jnp.abs(phi[:, None] - phi[None, :])
    phi_gap = jnp.minimum(phi_gap, PHI_CELLS - phi_gap)
    near = (eta_gap <= pair_reach) & (phi_gap <= 1)
    keep = jax.random.randint(key, (NB, NB), 0, 4) > 0
    full_line = (eta[:, None] == 5) | (eta[None, :] == 5)
    diagonal = index[:, None] == index[None, :]
    return jnp.where(near & (keep | full_line) | diagonal, 1, 0).astype(jnp.int32)


def block_levels(stream_key, extent, split, smallest, largest):
    gain, own = 1.0, jax.random.fold_in(stream_key, 6)
    for axis_at, blocks in split:
        steps = jnp.exp(jax.random.uniform(jax.random.fold_in(own, axis_at), (blocks,), jnp.float32, smallest / len(split), largest / len(split)))
        gain = gain * jnp.repeat(steps, extent[axis_at] // blocks).reshape([-1 if axis == axis_at else 1 for axis in range(len(extent))])
    return gain


def gaussian(stream_key, extent, scale, most, shards=(), held_as=jnp.bfloat16):
    gain = block_levels(stream_key, extent, shards, -0.22, 0.18) if shards else 1.0
    entries = jax.random.normal(stream_key, extent, jnp.float32) * scale * gain
    return jnp.minimum(jnp.maximum(entries, -most), most).astype(held_as)


def setup_inputs(seed: int = 0) -> dict:
    keys = jax.random.split(jax.random.key(seed), 9)
    return {
        "hits_in": draw_hits_in(jax.random.fold_in(keys[8], 71), 0),
        "w_query": gaussian(keys[1], (D, INNER), (1.4 * D ** -0.5), 0.25),
        "w_key": gaussian(keys[2], (D, INNER), (1.4 * D ** -0.5), 0.25),
        "w_value": gaussian(keys[3], (D, INNER), D ** -0.5, 0.1875),
        "w_out": gaussian(keys[4], (INNER, D), (2.0 * INNER ** -0.5), 0.5),
        "grad_y": gaussian(keys[5], (HITS, D), 1.0, 6.0, ((0, 256),)),
        "block_cell": jax.random.permutation(keys[6], NB).astype(jnp.int32),
        "cell_mask": draw_cell_mask(jax.random.fold_in(keys[8], 71), 0),
    }


def block_allowed(block_cell, cell_mask):
    amount = block_cell.shape[0]
    onehot = (block_cell[:, None] == jnp.arange(amount, dtype=jnp.int32)[None, :]).astype(jnp.float32)
    mask_table = cell_mask.astype(jnp.float32)
    picked = jnp.dot(onehot, mask_table, precision=lax.Precision.HIGHEST)
    return jnp.dot(picked, onehot.T, precision=lax.Precision.HIGHEST)


def block_lists(mask_rows):
    block_total = mask_rows.shape[1]
    is_live = mask_rows > 0.5
    slot_rank = jnp.cumsum(is_live.astype(jnp.int32), axis=1) - 1
    slot_ids = jnp.arange(KB_MAX, dtype=jnp.int32)
    matched = is_live[:, None, :] & (slot_rank[:, None, :] == slot_ids[None, :, None])
    positions = jnp.arange(block_total, dtype=jnp.int32)
    indices = jnp.sum(jnp.where(matched, positions[None, None, :], 0), axis=2).astype(jnp.int32)
    present = jnp.any(matched, axis=2)
    return indices, present


def rounded(values):
    return lax.optimization_barrier(values.astype(jnp.bfloat16))


def reference(hits_in, w_query, w_key, w_value, w_out, grad_y, block_cell, cell_mask):
    score_scale = HEAD_DIM ** -0.5
    total_hits = hits_in.shape[0]
    block_total = total_hits // BLOCK
    span = KB_MAX * BLOCK
    query = jnp.dot(hits_in, w_query, preferred_element_type=jnp.float32).astype(jnp.bfloat16)
    key = jnp.dot(hits_in, w_key, preferred_element_type=jnp.float32).astype(jnp.bfloat16)
    value = jnp.dot(hits_in, w_value, preferred_element_type=jnp.float32).astype(jnp.bfloat16)
    grad_attended = jnp.dot(grad_y, w_out.T, preferred_element_type=jnp.float32).astype(jnp.bfloat16)
    allowed = block_allowed(block_cell, cell_mask)
    key_index, key_present = block_lists(allowed)
    visible_all = jnp.repeat(key_present, BLOCK, axis=1)

    def split_heads(array):
        return array.reshape(block_total, BLOCK, HEADS, HEAD_DIM).transpose(2, 0, 1, 3)

    def head_pass(operands):
        query_wide = operands[0].astype(jnp.float32)
        key_wide = operands[1].astype(jnp.float32)
        value_wide = operands[2].astype(jnp.float32)
        grad_wide = operands[3].astype(jnp.float32)

        def one_block(sums, index):
            key_sum, value_sum = sums
            query_block = lax.dynamic_index_in_dim(query_wide, index, 0, keepdims=False)
            grad_block = lax.dynamic_index_in_dim(grad_wide, index, 0, keepdims=False)
            picks = lax.dynamic_index_in_dim(key_index, index, 0, keepdims=False)
            visible = lax.dynamic_index_in_dim(visible_all, index, 0, keepdims=False)[None, :]
            key_sel = key_wide[picks].reshape(span, HEAD_DIM)
            value_sel = value_wide[picks].reshape(span, HEAD_DIM)
            scores = jnp.dot(query_block, key_sel.T) * score_scale
            row_top = jnp.max(jnp.where(visible, scores, -jnp.inf), axis=1)
            norm_sum = jnp.sum(jnp.where(visible, jnp.exp(scores - row_top[:, None]), 0.0), axis=1)
            log_norm = row_top + jnp.log(norm_sum)
            probs = jnp.where(visible, jnp.exp(scores - log_norm[:, None]), 0.0)
            probs_low = rounded(probs).astype(jnp.float32)
            attended = rounded(jnp.dot(probs_low, value_sel))
            row_delta = jnp.sum(grad_block * attended.astype(jnp.float32), axis=1)
            dprobs = jnp.dot(grad_block, value_sel.T)
            dscores = rounded(probs * (dprobs - row_delta[:, None])).astype(jnp.float32)
            grad_query = (jnp.dot(dscores, key_sel) * score_scale).astype(jnp.bfloat16)
            key_term = (jnp.dot(dscores.T, query_block) * score_scale).reshape(KB_MAX, BLOCK, HEAD_DIM)
            value_term = jnp.dot(probs_low.T, grad_block).reshape(KB_MAX, BLOCK, HEAD_DIM)
            key_sum = key_sum.at[picks].add(key_term)
            value_sum = value_sum.at[picks].add(value_term)
            return (key_sum, value_sum), (attended, grad_query)

        zeros = jnp.zeros((block_total, BLOCK, HEAD_DIM), jnp.float32)
        sums, blocks = lax.scan(one_block, (zeros, zeros), jnp.arange(block_total, dtype=jnp.int32))
        return blocks[0], blocks[1], sums[0].astype(jnp.bfloat16), sums[1].astype(jnp.bfloat16)

    results = lax.map(head_pass, (split_heads(query), split_heads(key), split_heads(value), split_heads(grad_attended)))

    def join_heads(array):
        return array.transpose(1, 2, 0, 3).reshape(total_hits, HEADS * HEAD_DIM)

    attended_all = join_heads(results[0])
    layer_out = jnp.dot(attended_all, w_out, preferred_element_type=jnp.float32).astype(jnp.bfloat16)
    grad_hits = jnp.dot(join_heads(results[1]), w_query.T, preferred_element_type=jnp.float32)
    grad_hits = grad_hits + jnp.dot(join_heads(results[2]), w_key.T, preferred_element_type=jnp.float32)
    grad_hits = grad_hits + jnp.dot(join_heads(results[3]), w_value.T, preferred_element_type=jnp.float32)
    return layer_out, grad_hits.astype(jnp.bfloat16)
```

```python
import functools

import jax
import jax.numpy as jnp
from jax import lax
from jax.experimental import pallas as pl
from jax.experimental.pallas import tpu as pltpu
from jax.sharding import PartitionSpec as P

HEADS = 8
HEAD_DIM = 64
BLOCK = 128
KB_MAX = 21
CHUNK = 7
SCALE = HEAD_DIM ** (-0.5)
F32 = jnp.float32
BF16 = jnp.bfloat16
VMEM_LIMIT = 56 * 1024 * 1024

VMEM = pltpu.VMEM
NT = (((1,), (1,)), ((), ()))


def low_lanes(shape):
    return lax.broadcasted_iota(jnp.int32, shape, len(shape) - 1) < HEAD_DIM


def pack_heads(left, right, out_ref):
    for h in range(HEADS):
        cols = slice(h * HEAD_DIM, (h + 1) * HEAD_DIM)
        out_ref[h] = jnp.concatenate([left[:, cols], right[:, cols]], axis=1)


def project_kv_kernel(x_ref, wk_ref, wv_ref, out_ref):
    x = x_ref[...]
    k = jnp.dot(x, wk_ref[...], preferred_element_type=F32).astype(BF16)
    v = jnp.dot(x, wv_ref[...], preferred_element_type=F32).astype(BF16)
    pack_heads(k, v, out_ref)


def project_qd_kernel(x_ref, gy_ref, wq_ref, wo_ref, out_ref):
    q = jnp.dot(x_ref[...], wq_ref[...], preferred_element_type=F32).astype(BF16)
    q = q * jnp.asarray(SCALE, BF16)
    d = lax.dot_general(gy_ref[...], wo_ref[...], NT, preferred_element_type=F32).astype(BF16)
    pack_heads(q, d, out_ref)


def local_call(kernel, out_shape, n_in, **kw):
    return pl.pallas_call(
        kernel,
        out_shape=out_shape,
        in_specs=[pl.BlockSpec(memory_space=VMEM)] * n_in,
        out_specs=jax.tree.map(lambda _: pl.BlockSpec(memory_space=VMEM), out_shape),
        compiler_params=pltpu.CompilerParams(vmem_limit_bytes=VMEM_LIMIT),
        **kw,
    )


def load_pieces(pieces, dst, sems):
    copies = []
    at = 0
    for i, piece in enumerate(pieces):
        rows = piece.shape[0]
        copies.append(pltpu.make_async_copy(piece, dst.at[pl.ds(at, rows)], sems.at[i]))
        at += rows
    for copy in copies:
        copy.start()
    for copy in copies:
        copy.wait()


def query_kernel(n_pieces, blocks, pos_ref, cnt_ref, qd_ref, *rest):
    pieces = rest[:n_pieces]
    out_ref, stat_ref, kv_all, kv_pick, sems = rest[n_pieces:]
    load_pieces(pieces, kv_all, sems)
    span = KB_MAX * BLOCK

    def one(b, carry):
        for s in range(KB_MAX):
            at = pl.multiple_of(pos_ref[b, s] * BLOCK, BLOCK)
            kv_pick[pl.ds(s * BLOCK, BLOCK), :] = kv_all[pl.ds(at, BLOCK), :]
        rows = pl.ds(pl.multiple_of(b * BLOCK, BLOCK), BLOCK)
        qd = qd_ref[rows, :]
        low = low_lanes((BLOCK, 2 * HEAD_DIM))
        zero = jnp.zeros_like(qd)
        d_part = jnp.where(low, zero, qd)
        both = jnp.concatenate([jnp.where(low, qd, zero), d_part], axis=0)
        kv = kv_pick[...]
        prod = lax.dot_general(both, kv, NT, preferred_element_type=F32)
        slot = lax.broadcasted_iota(jnp.int32, (1, span), 1) // BLOCK
        scores = jnp.where(slot < cnt_ref[b], prod[:BLOCK], -1e30)
        top = jnp.max(scores, axis=1, keepdims=True)
        raw = jnp.exp(scores - top)
        total = jnp.sum(raw, axis=1, keepdims=True)
        probs = raw * (1.0 / total)
        probs_low = probs.astype(BF16)
        att = jnp.dot(probs_low, kv, preferred_element_type=F32)
        att_low = att.astype(BF16)
        delta = jnp.sum(d_part.astype(F32) * att_low.astype(F32), axis=1, keepdims=True)
        dscores = (probs * (prod[BLOCK:] - delta)).astype(BF16)
        gq = jnp.dot(dscores, kv, preferred_element_type=F32) * SCALE
        out_ref[b] = jnp.where(low, gq, att).astype(BF16)
        log_norm = top + jnp.log(total)
        lane = lax.broadcasted_iota(jnp.int32, (BLOCK, BLOCK), 1)
        tile = jnp.where(lane == 0, log_norm, delta)
        stat_ref[b] = jnp.transpose(tile)[:8]
        return carry

    lax.fori_loop(0, blocks, one, 0)


def query_side(pos, cnt, qd, pieces, blocks):
    n = len(pieces)
    rows = sum(p.shape[0] for p in pieces)
    smem = pl.BlockSpec(memory_space=pltpu.SMEM)
    vmem = pl.BlockSpec(memory_space=VMEM)
    return pl.pallas_call(
        functools.partial(query_kernel, n, blocks),
        out_shape=(
            jax.ShapeDtypeStruct((blocks, BLOCK, 2 * HEAD_DIM), BF16),
            jax.ShapeDtypeStruct((blocks, 8, BLOCK), F32),
        ),
        in_specs=[smem, smem, vmem] + [pl.BlockSpec(memory_space=pl.ANY)] * n,
        out_specs=(vmem, vmem),
        scratch_shapes=[
            pltpu.VMEM((rows, 2 * HEAD_DIM), BF16),
            pltpu.VMEM((KB_MAX * BLOCK, 2 * HEAD_DIM), BF16),
            pltpu.SemaphoreType.DMA((n,)),
        ],
        compiler_params=pltpu.CompilerParams(vmem_limit_bytes=VMEM_LIMIT),
        name="query_side",
    )(pos, cnt, qd, *pieces)


def key_kernel(n_pieces, blocks, pos_ref, cnt_ref, kv_ref, lse_ref, delta_ref, *rest):
    pieces = rest[:n_pieces]
    out_ref, qd_all, sems = rest[n_pieces:]
    load_pieces(pieces, qd_all, sems)

    def one(b, carry):
        rows = pl.ds(pl.multiple_of(b * BLOCK, BLOCK), BLOCK)
        kv = kv_ref[rows, :]
        low = low_lanes((BLOCK, 2 * HEAD_DIM))
        zero = jnp.zeros_like(kv)
        both = jnp.concatenate([jnp.where(low, kv, zero), jnp.where(low, zero, kv)], axis=0)
        cnt = cnt_ref[b]

        def chunk(c, acc):
            qds, lses, deltas = [], [], []
            for i in range(CHUNK):
                s = c * CHUNK + i
                at = pos_ref[b, s]
                qds.append(qd_all[pl.ds(pl.multiple_of(at * BLOCK, BLOCK), BLOCK), :])
                lses.append(jnp.where(s < cnt, lse_ref[pl.ds(at, 1), :], 1e30))
                deltas.append(delta_ref[pl.ds(at, 1), :])
            qd = jnp.concatenate(qds, axis=0)
            prod = lax.dot_general(both, qd, NT, preferred_element_type=F32)
            probs = jnp.exp(prod[:BLOCK] - jnp.concatenate(lses, axis=1))
            dscores = probs * (prod[BLOCK:] - jnp.concatenate(deltas, axis=1))
            left = jnp.concatenate([probs.astype(BF16), dscores.astype(BF16)], axis=0)
            return acc + jnp.dot(left, qd, preferred_element_type=F32)

        acc = lax.fori_loop(
            0, (cnt + CHUNK - 1) // CHUNK, chunk, jnp.zeros((2 * BLOCK, 2 * HEAD_DIM), F32)
        )
        out_ref[b] = jnp.where(low, acc[BLOCK:], acc[:BLOCK]).astype(BF16)
        return carry

    lax.fori_loop(0, blocks, one, 0)


def key_side(pos, cnt, kv, lse, delta, pieces, blocks):
    n = len(pieces)
    rows = sum(p.shape[0] for p in pieces)
    smem = pl.BlockSpec(memory_space=pltpu.SMEM)
    vmem = pl.BlockSpec(memory_space=VMEM)
    return pl.pallas_call(
        functools.partial(key_kernel, n, blocks),
        out_shape=jax.ShapeDtypeStruct((blocks, BLOCK, 2 * HEAD_DIM), BF16),
        in_specs=[smem, smem, vmem, vmem, vmem] + [pl.BlockSpec(memory_space=pl.ANY)] * n,
        out_specs=vmem,
        scratch_shapes=[
            pltpu.VMEM((rows, 2 * HEAD_DIM), BF16),
            pltpu.SemaphoreType.DMA((n,)),
        ],
        compiler_params=pltpu.CompilerParams(vmem_limit_bytes=VMEM_LIMIT),
        name="key_side",
    )(pos, cnt, kv, lse, delta, *pieces)


def unpack_heads(ref, left):
    cols = slice(0, HEAD_DIM) if left else slice(HEAD_DIM, 2 * HEAD_DIM)
    return jnp.concatenate([ref[h][:, cols] for h in range(HEADS)], axis=1)


def output_kernel(og_ref, wo_ref, wq_ref, out_ref, part_ref):
    att = unpack_heads(og_ref, False)
    gq = unpack_heads(og_ref, True)
    out_ref[...] = jnp.dot(att, wo_ref[...], preferred_element_type=F32).astype(BF16)
    part_ref[...] = lax.dot_general(gq, wq_ref[...], NT, preferred_element_type=F32)


def input_grad_kernel(kv_ref, part_ref, wk_ref, wv_ref, out_ref):
    gk = unpack_heads(kv_ref, True)
    gv = unpack_heads(kv_ref, False)
    total = part_ref[...] + lax.dot_general(gk, wk_ref[...], NT, preferred_element_type=F32)
    total = total + lax.dot_general(gv, wv_ref[...], NT, preferred_element_type=F32)
    out_ref[...] = total.astype(BF16)


def allowed_blocks(block_cell, cell_mask):
    amount = block_cell.shape[0]
    onehot = (block_cell[:, None] == jnp.arange(amount, dtype=jnp.int32)[None, :]).astype(BF16)
    picked = jnp.dot(onehot, cell_mask.astype(BF16), preferred_element_type=F32).astype(BF16)
    return lax.dot_general(picked, onehot, NT, preferred_element_type=F32)


def block_lists(rows, place):
    total = rows.shape[1]
    at = jnp.arange(total, dtype=jnp.int32)
    upto = (at[:, None] <= at[None, :]).astype(BF16)
    rank = jnp.dot(rows.astype(BF16), upto, preferred_element_type=F32)
    slots = jnp.arange(1, KB_MAX + 1, dtype=jnp.int32).astype(F32)
    matched = (rows[:, None, :] > 0.5) & (rank[:, None, :] == slots[None, :, None])
    picked = jnp.sum(jnp.where(matched, place[None, None, :], 0), axis=2)
    return picked, jnp.sum(rows, axis=1).astype(jnp.int32)


def exchange(x):
    return lax.all_to_all(x, "head", split_axis=0, concat_axis=0, tiled=True)


def body(hits_in, w_query, w_key, w_value, w_out, grad_y, block_cell, cell_mask):
    rows = hits_in.shape[0]
    own_blocks = HEADS * rows // BLOCK
    wide = 2 * HEAD_DIM
    packed = jax.ShapeDtypeStruct((HEADS, rows, wide), BF16)
    kv = exchange(local_call(project_kv_kernel, packed, 3)(hits_in, w_key, w_value))
    qd = exchange(local_call(project_qd_kernel, packed, 4)(hits_in, grad_y, w_query, w_out))
    kv = kv.reshape(own_blocks * BLOCK, wide)
    qd = qd.reshape(own_blocks * BLOCK, wide)
    kv_all = lax.all_gather(kv, "ctx", axis=0, tiled=True)
    qd_all = lax.all_gather(qd, "ctx", axis=0, tiled=True)

    allowed = allowed_blocks(block_cell, cell_mask)
    first = lax.axis_index("ctx") * own_blocks
    place = jnp.arange(allowed.shape[0], dtype=jnp.int32)
    lists = jnp.concatenate(
        [
            lax.dynamic_slice_in_dim(allowed, first, own_blocks, 0),
            lax.dynamic_slice_in_dim(allowed, first, own_blocks, 1).T,
        ],
        axis=0,
    )
    pos, cnt = block_lists(lists, place)

    og, stats = query_side(pos[:own_blocks], cnt[:own_blocks], qd, [kv_all], own_blocks)
    both = jnp.concatenate([stats[:, 0], stats[:, 1]], axis=1)
    both = lax.all_gather(both, "ctx", axis=0, tiled=True)
    og = exchange(og.reshape(HEADS, rows, wide))
    layer_out, part = local_call(
        output_kernel,
        (
            jax.ShapeDtypeStruct(hits_in.shape, BF16),
            jax.ShapeDtypeStruct(hits_in.shape, F32),
        ),
        3,
    )(og, w_out, w_query)
    gkv = key_side(
        pos[own_blocks:], cnt[own_blocks:], kv, both[:, :BLOCK], both[:, BLOCK:], [qd_all], own_blocks
    )
    gkv = exchange(gkv.reshape(HEADS, rows, wide))
    grad_hits = local_call(
        input_grad_kernel, jax.ShapeDtypeStruct(hits_in.shape, BF16), 4
    )(gkv, part, w_key, w_value)
    return layer_out, grad_hits


def solution(mesh):
    row = P(("ctx", "head"), None)
    return jax.shard_map(
        body,
        mesh=mesh,
        in_specs=(row, P(), P(), P(), P(), row, P(), P()),
        out_specs=(row, row),
        check_vma=False,
    )
```

```python
import functools

import jax
import jax.numpy as jnp
from jax import lax
from jax.experimental import pallas as pl
from jax.experimental.pallas import tpu as pltpu
from jax.sharding import PartitionSpec as P

HEADS = 8
HEAD_DIM = 64
WIDE = 2 * HEAD_DIM
BLOCK = 128
KB_MAX = 21
CHUNK = 4
SLOTS = -(-KB_MAX // CHUNK) * CHUNK
LINE = 4
CORES = 2
OWN = 8
Q_BLOCKS = LINE * OWN
K_BLOCKS = LINE * CORES * OWN
HOPS = (0, 1, -1, 2)
SCALE = HEAD_DIM ** (-0.5)
FAR = -1e30
F32 = jnp.float32
BF16 = jnp.bfloat16
VMEM_LIMIT = 56 * 1024 * 1024

VMEM = pl.BlockSpec(memory_space=pltpu.VMEM)
SMEM = pl.BlockSpec(memory_space=pltpu.SMEM)
ANY = pl.BlockSpec(memory_space=pl.ANY)
NT = (((1,), (1,)), ((), ()))
TN = (((0,), (0,)), ((), ()))


def call(kernel, out_shape, in_specs, scratch=(), name=None):
    return pl.pallas_call(
        kernel,
        out_shape=out_shape,
        in_specs=in_specs,
        out_specs=jax.tree.map(lambda _: VMEM, out_shape),
        scratch_shapes=scratch,
        compiler_params=pltpu.CompilerParams(vmem_limit_bytes=VMEM_LIMIT),
        name=name,
    )


def struct(shape, dtype):
    return jax.ShapeDtypeStruct(shape, dtype)


def project_kernel(x_ref, gy_ref, wq_ref, wk_ref, wv_ref, wo_ref, out_ref):
    x = x_ref[...]
    k = jnp.dot(x, wk_ref[...], preferred_element_type=F32).astype(BF16)
    v = jnp.dot(x, wv_ref[...], preferred_element_type=F32).astype(BF16)
    q = jnp.dot(x, wq_ref[...], preferred_element_type=F32).astype(BF16)
    q = q * jnp.asarray(SCALE, BF16)
    d = lax.dot_general(gy_ref[...], wo_ref[...], NT, preferred_element_type=F32).astype(BF16)
    for h in range(HEADS):
        cols = slice(h * HEAD_DIM, (h + 1) * HEAD_DIM)
        out_ref[h, :BLOCK] = jnp.concatenate([k[:, cols], v[:, cols]], axis=1)
        out_ref[h, BLOCK:] = jnp.concatenate([q[:, cols], d[:, cols]], axis=1)


def line_of(hop, at):
    return (at - hop + LINE) % LINE


def load_lines(me_ref, kv_pieces, qd_pieces, kv_all, qd_all, sems):
    y, x, c = me_ref[0], me_ref[1], me_ref[2]
    copies = []
    rows = OWN * BLOCK
    for i, piece in enumerate(kv_pieces):
        hop, other = HOPS[i % LINE], i // LINE
        core = c if other == 0 else 1 - c
        at = pl.multiple_of((line_of(hop, x) * CORES + core) * rows, rows)
        copies.append(pltpu.make_async_copy(piece, kv_all.at[pl.ds(at, rows)], sems.at[i]))
    for i, piece in enumerate(qd_pieces):
        at = pl.multiple_of(line_of(HOPS[i], y) * rows, rows)
        copies.append(
            pltpu.make_async_copy(piece, qd_all.at[pl.ds(at, rows)], sems.at[len(kv_pieces) + i])
        )
    for copy in copies:
        copy.start()
    for copy in copies:
        copy.wait()


def query_pair(qd_all, b):
    qd = qd_all[pl.ds(pl.multiple_of(b * BLOCK, BLOCK), BLOCK), :]
    low = lax.broadcasted_iota(jnp.int32, qd.shape, 1) < HEAD_DIM
    zero = jnp.zeros_like(qd)
    return jnp.concatenate([jnp.where(low, qd, zero), jnp.where(low, zero, qd)], axis=0)


def chunk_products(pos_ref, kv_all, pair, b, c, cnt):
    kvs, far = [], []
    for i in range(CHUNK):
        s = c * CHUNK + i
        at = pl.multiple_of(pos_ref[b, s] * BLOCK, BLOCK)
        kvs.append(kv_all[pl.ds(at, BLOCK), :])
        far.append(jnp.where(s < cnt, 0.0, FAR))
    kv = jnp.concatenate(kvs, axis=0)
    prod = lax.dot_general(kv, pair, NT, preferred_element_type=F32)
    scores = jnp.concatenate(
        [prod[i * BLOCK : (i + 1) * BLOCK, :BLOCK] + far[i] for i in range(CHUNK)], axis=0
    )
    return kv, scores, prod[:, BLOCK:]


def chunks_of(cnt):
    return (cnt + CHUNK - 1) // CHUNK


def stats_kernel(me_ref, pos_ref, cnt_ref, *rest):
    kv_pieces, qd_pieces = rest[: 2 * LINE], rest[2 * LINE : 3 * LINE]
    top_ref, kv_all, qd_all, sems = rest[3 * LINE :]
    load_lines(me_ref, kv_pieces, qd_pieces, kv_all, qd_all, sems)

    def one(b, carry):
        pair = query_pair(qd_all, b)
        cnt = cnt_ref[b]

        def chunk(c, state):
            top, total, dot = state
            _, scores, dprobs = chunk_products(pos_ref, kv_all, pair, b, c, cnt)
            new = jnp.maximum(top, jnp.max(scores, axis=0, keepdims=True))
            keep = jnp.exp(top - new)
            raw = jnp.exp(scores - new)
            total = total * keep + jnp.sum(raw, axis=0, keepdims=True)
            dot = dot * keep + jnp.sum(raw * dprobs, axis=0, keepdims=True)
            return new, total, dot

        zero = jnp.zeros((1, BLOCK), F32)
        top, total, dot = lax.fori_loop(
            0, chunks_of(cnt), chunk, (jnp.full((1, BLOCK), FAR, F32), zero, zero)
        )
        top_ref[0, pl.ds(b, 1), :] = top
        top_ref[1, pl.ds(b, 1), :] = total
        top_ref[2, pl.ds(b, 1), :] = dot
        return carry

    lax.fori_loop(0, Q_BLOCKS, one, 0)


def grads_kernel(me_ref, pos_ref, cnt_ref, *rest):
    stats, rest = rest[:LINE], rest[LINE:]
    kv_pieces, qd_pieces, rest = rest[: 2 * LINE], rest[2 * LINE : 3 * LINE], rest[3 * LINE :]
    y_refs, rest = rest[:LINE], rest[LINE:]
    own_ref, other_ref, kv_all, qd_all, acc_ref, lse_ref, delta_ref, sems = rest
    load_lines(me_ref, kv_pieces, qd_pieces, kv_all, qd_all, sems)

    top = functools.reduce(jnp.maximum, [s[0] for s in stats])
    weights = [jnp.exp(s[0] - top) for s in stats]
    total = sum(s[1] * w for s, w in zip(stats, weights))
    dot = sum(s[2] * w for s, w in zip(stats, weights))
    lse_ref[...] = top + jnp.log(total)
    delta_ref[...] = dot / total
    acc_ref[...] = jnp.zeros_like(acc_ref)
    y = me_ref[0]

    def one(n, carry):
        hop_at, i = n // OWN, n % OWN
        hop = jnp.where(hop_at == 3, 2, jnp.where(hop_at == 2, -1, hop_at))
        b = (y + hop + LINE) % LINE * OWN + i
        pair = query_pair(qd_all, b)
        cnt = cnt_ref[b]
        lse = lse_ref[pl.ds(b, 1), :]
        delta = delta_ref[pl.ds(b, 1), :]

        def chunk(c, state):
            kv, scores, dprobs = chunk_products(pos_ref, kv_all, pair, b, c, cnt)
            probs = jnp.exp(scores - lse)
            dscores = probs * (dprobs - delta)
            low = jnp.concatenate([dscores.astype(BF16), probs.astype(BF16)], axis=1)
            terms = jnp.dot(low, pair, preferred_element_type=F32)
            for s in range(CHUNK):
                at = pos_ref[b, c * CHUNK + s]
                acc_ref[at] = acc_ref[at] + terms[s * BLOCK : (s + 1) * BLOCK]
            return state + lax.dot_general(kv, low, TN, preferred_element_type=F32)

        state = lax.fori_loop(0, chunks_of(cnt), chunk, jnp.zeros((WIDE, 2 * BLOCK), F32))
        out = jnp.concatenate([state[:HEAD_DIM, :BLOCK] * SCALE, state[HEAD_DIM:, BLOCK:]], axis=0)
        for k in range(LINE):

            @pl.when(hop_at == k)
            def _():
                y_refs[k][i] = out.astype(y_refs[k].dtype)

        return carry

    lax.fori_loop(0, Q_BLOCKS, one, 0)
    core = me_ref[2]

    def spread(n, carry):
        line, i = n // OWN, n % OWN
        own_ref[n] = acc_ref[(line * CORES + core) * OWN + i]
        other_ref[n] = acc_ref[(line * CORES + 1 - core) * OWN + i].astype(BF16)
        return carry

    lax.fori_loop(0, LINE * OWN, spread, 0)


def core_sum_kernel(me_ref, own_ref, other_ref, *out_refs):
    x = me_ref[1]
    for k, hop in enumerate(HOPS):
        line = (x + hop + LINE) % LINE
        rows = pl.ds(line * OWN, OWN)
        out_refs[k][...] = (own_ref[rows] + other_ref[rows].astype(F32)).astype(out_refs[k].dtype)


def line_sum_kernel(*refs):
    xs, ys, out_ref = refs[:LINE], refs[LINE : 2 * LINE], refs[2 * LINE]
    for at, parts in ((0, xs), (BLOCK, ys)):
        total = sum(p[...].astype(F32) for p in parts)
        out_ref[:, at : at + BLOCK] = total.astype(BF16)


def output_kernel(in_ref, wq_ref, wk_ref, wv_ref, wo_ref, out_ref, grad_ref):
    gk = jnp.concatenate([in_ref[h, :BLOCK, :HEAD_DIM] for h in range(HEADS)], axis=1)
    gv = jnp.concatenate([in_ref[h, :BLOCK, HEAD_DIM:] for h in range(HEADS)], axis=1)
    gq = jnp.concatenate([in_ref[h, BLOCK : BLOCK + HEAD_DIM] for h in range(HEADS)], axis=0)
    att = jnp.concatenate([in_ref[h, BLOCK + HEAD_DIM :] for h in range(HEADS)], axis=0)
    out = lax.dot_general(att, wo_ref[...], TN, preferred_element_type=F32)
    out_ref[...] = out.astype(BF16)
    total = lax.dot_general(
        gq, wq_ref[...], (((0,), (1,)), ((), ())), preferred_element_type=F32
    )
    total = total + lax.dot_general(gk, wk_ref[...], NT, preferred_element_type=F32)
    total = total + lax.dot_general(gv, wv_ref[...], NT, preferred_element_type=F32)
    grad_ref[...] = total.astype(BF16)


def ctx_shift(x, dy=0, dx=0, dc=0):
    pairs = []
    for i in range(LINE * LINE * CORES):
        y, r, c = i // (LINE * CORES), i // CORES % LINE, i % CORES
        to = ((y + dy) % LINE * LINE + (r + dx) % LINE) * CORES + (c + dc) % CORES
        pairs.append((i, to))
    return lax.ppermute(x, "ctx", pairs)


def live_lists(block_cell, cell_mask, y, xc):
    cells = jnp.arange(cell_mask.shape[0], dtype=jnp.int32)
    by_line = block_cell.reshape(LINE, LINE * CORES, OWN)
    q_cell = lax.dynamic_index_in_dim(by_line, xc, 1, keepdims=False).reshape(Q_BLOCKS)
    k_cell = lax.dynamic_slice_in_dim(block_cell, y * K_BLOCKS, K_BLOCKS, 0)
    q_hot = (q_cell[:, None] == cells[None, :]).astype(BF16)
    k_hot = (k_cell[:, None] == cells[None, :]).astype(BF16)
    picked = jnp.dot(q_hot, cell_mask.astype(BF16), preferred_element_type=F32).astype(BF16)
    live = lax.dot_general(picked, k_hot, NT, preferred_element_type=F32)
    at = jnp.arange(K_BLOCKS, dtype=jnp.int32)
    upto = (at[:, None] <= at[None, :]).astype(BF16)
    rank = jnp.dot(live.astype(BF16), upto, preferred_element_type=F32)
    slots = jnp.arange(1, SLOTS + 1, dtype=jnp.int32).astype(F32)
    matched = (live[:, None, :] > 0.5) & (rank[:, None, :] == slots[None, :, None])
    pos = jnp.sum(jnp.where(matched, at[None, None, :], 0), axis=2)
    return pos, jnp.sum(live, axis=1).astype(jnp.int32)


def exchange(x):
    return lax.all_to_all(x, "head", split_axis=0, concat_axis=0, tiled=True)


def body(hits_in, w_query, w_key, w_value, w_out, grad_y, block_cell, cell_mask):
    rows = OWN * BLOCK
    ctx = lax.axis_index("ctx")
    y, x, core = ctx // (LINE * CORES), ctx // CORES % LINE, ctx % CORES
    me = jnp.stack([y, x, core]).astype(jnp.int32)
    pos, cnt = live_lists(block_cell, cell_mask, y, ctx % (LINE * CORES))

    sent = call(project_kernel, struct((HEADS, 2 * BLOCK, WIDE), BF16), [VMEM] * 6, name="project")(
        hits_in, grad_y, w_query, w_key, w_value, w_out
    )
    got = exchange(sent)
    kv = got[:, :BLOCK].reshape(rows, WIDE)
    qd = got[:, BLOCK:].reshape(rows, WIDE)
    kvs = [kv] + [ctx_shift(kv, dx=hop) for hop in HOPS[1:]]
    kvs = kvs + [ctx_shift(piece, dc=1) for piece in kvs]
    qds = [qd] + [ctx_shift(qd, dy=hop) for hop in HOPS[1:]]

    lines = [pltpu.VMEM((K_BLOCKS * BLOCK, WIDE), BF16), pltpu.VMEM((Q_BLOCKS * BLOCK, WIDE), BF16)]
    sems = pltpu.SemaphoreType.DMA((3 * LINE,))
    stats = call(
        stats_kernel,
        struct((3, Q_BLOCKS, BLOCK), F32),
        [SMEM] * 3 + [ANY] * (3 * LINE),
        lines + [sems],
        "stats",
    )(me, pos, cnt, *kvs, *qds)
    all_stats = [stats] + [ctx_shift(stats, dy=hop) for hop in HOPS[1:]]

    tile = (OWN, BLOCK, WIDE)
    mixed = [struct(tile, F32)] + [struct(tile, BF16)] * (LINE - 1)
    *y_parts, own, other = call(
        grads_kernel,
        mixed + [struct((LINE * OWN, BLOCK, WIDE), F32), struct((LINE * OWN, BLOCK, WIDE), BF16)],
        [SMEM] * 3 + [VMEM] * LINE + [ANY] * (3 * LINE),
        lines
        + [pltpu.VMEM((K_BLOCKS, BLOCK, WIDE), F32)]
        + [pltpu.VMEM((Q_BLOCKS, BLOCK), F32)] * 2
        + [sems],
        "grads",
    )(me, pos, cnt, *all_stats, *kvs, *qds)
    y_parts = [y_parts[0]] + [ctx_shift(p, dy=hop) for p, hop in zip(y_parts[1:], HOPS[1:])]
    other = ctx_shift(other, dc=1)
    x_parts = call(core_sum_kernel, mixed, [SMEM, VMEM, VMEM], name="core_sum")(me, own, other)
    x_parts = [x_parts[0]] + [ctx_shift(p, dx=hop) for p, hop in zip(x_parts[1:], HOPS[1:])]
    summed = call(
        line_sum_kernel, struct((HEADS, 2 * BLOCK, WIDE), BF16), [VMEM] * (2 * LINE), name="line_sum"
    )(*x_parts, *y_parts)
    back = exchange(summed)
    full = struct(hits_in.shape, BF16)
    return call(output_kernel, (full, full), [VMEM] * 5, name="output")(
        back, w_query, w_key, w_value, w_out
    )


def solution(mesh):
    row = P(("ctx", "head"), None)
    return jax.shard_map(
        body,
        mesh=mesh,
        in_specs=(row, P(), P(), P(), P(), row, P(), P()),
        out_specs=(row, row),
        check_vma=False,
    )
```

```python
import functools

import jax
import jax.numpy as jnp
from jax import lax
from jax.experimental import pallas as pl
from jax.experimental.pallas import tpu as pltpu
from jax.sharding import PartitionSpec as P

HEADS = 8
HEAD_DIM = 64
WIDE = 2 * HEAD_DIM
BLOCK = 128
KB_MAX = 21
SLOTS = 24
STATS_ITEM = 2
GRADS_ITEM = 4
STATS_UNROLL = 8
GRADS_UNROLL = 4
LINE = 4
CORES = 2
OWN = 8
Q_BLOCKS = LINE * OWN
K_BLOCKS = LINE * CORES * OWN
HOPS = (0, 1, -1, 2)
SCALE = HEAD_DIM ** (-0.5)
FAR = -1e30
F32 = jnp.float32
BF16 = jnp.bfloat16
VMEM_LIMIT = 32 * 1024 * 1024

VMEM = pl.BlockSpec(memory_space=pltpu.VMEM)
SMEM = pl.BlockSpec(memory_space=pltpu.SMEM)
ANY = pl.BlockSpec(memory_space=pl.ANY)
NT = (((1,), (1,)), ((), ()))
TN = (((0,), (0,)), ((), ()))


def call(kernel, out_shape, in_specs, scratch=(), name=None):
    return pl.pallas_call(
        kernel,
        out_shape=out_shape,
        in_specs=in_specs,
        out_specs=jax.tree.map(lambda _: VMEM, out_shape),
        scratch_shapes=scratch,
        compiler_params=pltpu.CompilerParams(vmem_limit_bytes=VMEM_LIMIT),
        name=name,
    )


def struct(shape, dtype):
    return jax.ShapeDtypeStruct(shape, dtype)


def near(*arrays):
    return [pltpu.with_memory_space_constraint(a, pltpu.VMEM) for a in arrays]


def project_kernel(*refs):
    out_ref, bufs, sems = refs[6], refs[7:13], refs[13]
    copies = [pltpu.make_async_copy(refs[i], bufs[i], sems.at[i]) for i in range(6)]
    for copy in copies:
        copy.start()

    def arrived(i):
        copies[i].wait()
        return bufs[i][...]

    x = arrived(0)
    k = jnp.dot(x, arrived(1), preferred_element_type=F32).astype(BF16)
    v = jnp.dot(x, arrived(2), preferred_element_type=F32).astype(BF16)
    q = jnp.dot(x, arrived(3), preferred_element_type=F32).astype(BF16)
    q = q * jnp.asarray(SCALE, BF16)
    gy = arrived(4)
    d = lax.dot_general(gy, arrived(5), NT, preferred_element_type=F32).astype(BF16)
    for h in range(HEADS):
        cols = slice(h * HEAD_DIM, (h + 1) * HEAD_DIM)
        out_ref[h, :BLOCK] = jnp.concatenate([k[:, cols], v[:, cols]], axis=1)
        out_ref[h, BLOCK:] = jnp.concatenate([q[:, cols], d[:, cols]], axis=1)


def line_of(hop, at):
    return (at - hop + LINE) % LINE


def load_lines(me_ref, kv_pieces, qd_pieces, kv_all, qd_all, sems):
    y, x, c = me_ref[0], me_ref[1], me_ref[2]
    copies = []
    rows = OWN * BLOCK
    for i, piece in enumerate(kv_pieces):
        hop, other = HOPS[i % LINE], i // LINE
        core = c if other == 0 else 1 - c
        at = pl.multiple_of((line_of(hop, x) * CORES + core) * rows, rows)
        copies.append(pltpu.make_async_copy(piece, kv_all.at[pl.ds(at, rows)], sems.at[i]))
    for i, piece in enumerate(qd_pieces):
        at = pl.multiple_of(line_of(HOPS[i], y) * rows, rows)
        copies.append(
            pltpu.make_async_copy(piece, qd_all.at[pl.ds(at, rows)], sems.at[len(kv_pieces) + i])
        )
    for copy in copies:
        copy.start()
    return copies


def query_pair(qd_all, b):
    qd = qd_all[pl.ds(pl.multiple_of(b * BLOCK, BLOCK), BLOCK), :]
    low = lax.broadcasted_iota(jnp.int32, qd.shape, 1) < HEAD_DIM
    zero = jnp.zeros_like(qd)
    return jnp.concatenate([jnp.where(low, qd, zero), jnp.where(low, zero, qd)], axis=0)


def build_items(cnt_ref, item_ref, size):
    def one(b, at):
        def put(j, at):
            item_ref[at] = b * 16 + j
            return at + 1

        return lax.fori_loop(0, (cnt_ref[b] + size - 1) // size, put, at)

    return lax.fori_loop(0, Q_BLOCKS, one, 0)


def read_item(item_ref, pos_ref, cnt_ref, at, amount, size):
    code = item_ref[jnp.minimum(at, amount - 1)]
    b, j = code // 16, code % 16
    limit = jnp.where(at < amount, cnt_ref[b], 0)
    places = [pos_ref[b, size * j + s] for s in range(size)]
    far = [jnp.where(size * j + s < limit, 0.0, FAR) for s in range(size)]
    return b, places, far


def item_products(kv_all, pair, places, far):
    kv = jnp.concatenate(
        [kv_all[pl.ds(pl.multiple_of(p * BLOCK, BLOCK), BLOCK), :] for p in places], axis=0
    )
    prod = lax.dot_general(kv, pair, NT, preferred_element_type=F32)
    scores = jnp.concatenate(
        [prod[s * BLOCK : (s + 1) * BLOCK, :BLOCK] + far[s] for s in range(len(places))], axis=0
    )
    return kv, scores, prod[:, BLOCK:]


def stats_kernel(me_ref, pos_ref, cnt_ref, *rest):
    kv_pieces, qd_pieces = rest[: 2 * LINE], rest[2 * LINE : 3 * LINE]
    out_ref, kv_all, qd_all, item_ref, sems = rest[3 * LINE :]
    copies = load_lines(me_ref, kv_pieces, qd_pieces, kv_all, qd_all, sems)
    out_ref[0] = jnp.full((Q_BLOCKS, BLOCK), FAR, F32)
    out_ref[1:] = jnp.zeros((2, Q_BLOCKS, BLOCK), F32)
    amount = build_items(cnt_ref, item_ref, STATS_ITEM)
    for copy in copies:
        copy.wait()

    def step(n, carry):
        done = []
        for u in range(STATS_UNROLL):
            at = n * STATS_UNROLL + u
            b, places, far = read_item(item_ref, pos_ref, cnt_ref, at, amount, STATS_ITEM)
            _, scores, dprobs = item_products(kv_all, query_pair(qd_all, b), places, far)
            top = jnp.max(scores, axis=0, keepdims=True)
            raw = jnp.exp(scores - top)
            total = jnp.sum(raw, axis=0, keepdims=True)
            dot = jnp.sum(raw * dprobs, axis=0, keepdims=True)
            done.append((pl.ds(b, 1), top, total, dot))
        for row, top, total, dot in done:
            old = out_ref[0, row, :]
            new = jnp.maximum(old, top)
            keep, take = jnp.exp(old - new), jnp.exp(top - new)
            out_ref[0, row, :] = new
            out_ref[1, row, :] = out_ref[1, row, :] * keep + total * take
            out_ref[2, row, :] = out_ref[2, row, :] * keep + dot * take
        return carry

    lax.fori_loop(0, (amount + STATS_UNROLL - 1) // STATS_UNROLL, step, 0)


def grads_kernel(me_ref, pos_ref, cnt_ref, *rest):
    stats, rest = rest[:LINE], rest[LINE:]
    kv_pieces, qd_pieces, rest = rest[: 2 * LINE], rest[2 * LINE : 3 * LINE], rest[3 * LINE :]
    y_refs, rest = rest[:LINE], rest[LINE:]
    own_ref, other_ref, kv_all, qd_all, key_ref, query_ref, lse_ref, delta_ref, item_ref, sems = rest
    copies = load_lines(me_ref, kv_pieces, qd_pieces, kv_all, qd_all, sems)

    top = functools.reduce(jnp.maximum, [s[0] for s in stats])
    weights = [jnp.exp(s[0] - top) for s in stats]
    total = sum(s[1] * w for s, w in zip(stats, weights))
    dot = sum(s[2] * w for s, w in zip(stats, weights))
    lse_ref[...] = top + jnp.log(total)
    delta_ref[...] = dot / total
    key_ref[...] = jnp.zeros_like(key_ref)
    query_ref[...] = jnp.zeros_like(query_ref)
    amount = build_items(cnt_ref, item_ref, GRADS_ITEM)
    for copy in copies:
        copy.wait()

    def step(n, carry):
        done = []
        for u in range(GRADS_UNROLL):
            at = n * GRADS_UNROLL + u
            b, places, far = read_item(item_ref, pos_ref, cnt_ref, at, amount, GRADS_ITEM)
            pair = query_pair(qd_all, b)
            kv, scores, dprobs = item_products(kv_all, pair, places, far)
            probs = jnp.exp(scores - lse_ref[pl.ds(b, 1), :])
            dscores = probs * (dprobs - delta_ref[pl.ds(b, 1), :])
            low = jnp.concatenate([dscores.astype(BF16), probs.astype(BF16)], axis=1)
            terms = jnp.dot(low, pair, preferred_element_type=F32)
            mixed = lax.dot_general(kv, low, TN, preferred_element_type=F32)
            out = jnp.concatenate([mixed[:HEAD_DIM, :BLOCK], mixed[HEAD_DIM:, BLOCK:]], axis=0)
            done.append((b, places, terms, out))
        for b, places, terms, out in done:
            for s, p in enumerate(places):
                key_ref[p] = key_ref[p] + terms[s * BLOCK : (s + 1) * BLOCK]
            query_ref[b] = query_ref[b] + out
        return carry

    lax.fori_loop(0, (amount + GRADS_UNROLL - 1) // GRADS_UNROLL, step, 0)
    y, core = me_ref[0], me_ref[2]

    def spread(n, carry):
        line, i = n // OWN, n % OWN
        own_ref[n] = key_ref[(line * CORES + core) * OWN + i]
        other_ref[n] = key_ref[(line * CORES + 1 - core) * OWN + i].astype(BF16)
        return carry

    lax.fori_loop(0, LINE * OWN, spread, 0)
    for k, hop in enumerate(HOPS):
        line = (y + hop + LINE) % LINE * OWN

        def scaled(i, carry):
            out = query_ref[line + i]
            out = jnp.concatenate([out[:HEAD_DIM] * SCALE, out[HEAD_DIM:]], axis=0)
            y_refs[k][i] = out.astype(y_refs[k].dtype)
            return carry

        lax.fori_loop(0, OWN, scaled, 0)


def core_sum_kernel(me_ref, own_ref, other_ref, *out_refs):
    x = me_ref[1]
    for k, hop in enumerate(HOPS):
        line = (x + hop + LINE) % LINE
        rows = pl.ds(line * OWN, OWN)
        out_refs[k][...] = (own_ref[rows] + other_ref[rows].astype(F32)).astype(out_refs[k].dtype)


def line_sum_kernel(*refs):
    xs, ys, out_ref = refs[:LINE], refs[LINE : 2 * LINE], refs[2 * LINE]
    for at, parts in ((0, xs), (BLOCK, ys)):
        out_ref[:, at : at + BLOCK] = sum(p[...].astype(F32) for p in parts).astype(BF16)


def output_kernel(in_ref, wq_ref, wk_ref, wv_ref, wo_ref, out_ref, grad_ref):
    gk = jnp.concatenate([in_ref[h, :BLOCK, :HEAD_DIM] for h in range(HEADS)], axis=1)
    gv = jnp.concatenate([in_ref[h, :BLOCK, HEAD_DIM:] for h in range(HEADS)], axis=1)
    gq = jnp.concatenate([in_ref[h, BLOCK : BLOCK + HEAD_DIM] for h in range(HEADS)], axis=0)
    att = jnp.concatenate([in_ref[h, BLOCK + HEAD_DIM :] for h in range(HEADS)], axis=0)
    out = lax.dot_general(att, wo_ref[...], TN, preferred_element_type=F32)
    out_ref[...] = out.astype(BF16)
    total = lax.dot_general(
        gq, wq_ref[...], (((0,), (1,)), ((), ())), preferred_element_type=F32
    )
    total = total + lax.dot_general(gk, wk_ref[...], NT, preferred_element_type=F32)
    total = total + lax.dot_general(gv, wv_ref[...], NT, preferred_element_type=F32)
    grad_ref[...] = total.astype(BF16)


def ctx_shift(x, dy=0, dx=0, dc=0):
    pairs = []
    for i in range(LINE * LINE * CORES):
        y, r, c = i // (LINE * CORES), i // CORES % LINE, i % CORES
        to = ((y + dy) % LINE * LINE + (r + dx) % LINE) * CORES + (c + dc) % CORES
        pairs.append((i, to))
    return lax.ppermute(x, "ctx", pairs)


def live_lists(block_cell, cell_mask, y, xc):
    cells = jnp.arange(cell_mask.shape[0], dtype=jnp.int32)
    by_line = block_cell.reshape(LINE, LINE * CORES, OWN)
    q_cell = lax.dynamic_index_in_dim(by_line, xc, 1, keepdims=False).reshape(Q_BLOCKS)
    k_cell = lax.dynamic_slice_in_dim(block_cell, y * K_BLOCKS, K_BLOCKS, 0)
    q_hot = (q_cell[:, None] == cells[None, :]).astype(BF16)
    k_hot = (k_cell[:, None] == cells[None, :]).astype(BF16)
    picked = jnp.dot(q_hot, cell_mask.astype(BF16), preferred_element_type=F32).astype(BF16)
    live = lax.dot_general(picked, k_hot, NT, preferred_element_type=F32)
    at = jnp.arange(K_BLOCKS, dtype=jnp.int32)
    upto = (at[:, None] <= at[None, :]).astype(BF16)
    rank = jnp.dot(live.astype(BF16), upto, preferred_element_type=F32)
    slots = jnp.arange(1, SLOTS + 1, dtype=jnp.int32).astype(F32)
    matched = (live[:, None, :] > 0.5) & (rank[:, None, :] == slots[None, :, None])
    pos = jnp.sum(jnp.where(matched, at[None, None, :], 0), axis=2)
    return pos, jnp.sum(live, axis=1).astype(jnp.int32)


def exchange(x):
    return lax.all_to_all(x, "head", split_axis=0, concat_axis=0, tiled=True)


def scratch_lines():
    return [
        pltpu.VMEM((K_BLOCKS * BLOCK, WIDE), BF16),
        pltpu.VMEM((Q_BLOCKS * BLOCK, WIDE), BF16),
    ]


def scratch_work():
    return [pltpu.SMEM((Q_BLOCKS * SLOTS // STATS_ITEM,), jnp.int32), pltpu.SemaphoreType.DMA((3 * LINE,))]


MIXED = [struct((OWN, BLOCK, WIDE), F32)] + [struct((OWN, BLOCK, WIDE), BF16)] * (LINE - 1)


def stats_call(me, pos, cnt, kvs, qds):
    return call(
        stats_kernel,
        struct((3, Q_BLOCKS, BLOCK), F32),
        [SMEM] * 3 + [VMEM] * (3 * LINE),
        scratch_lines() + scratch_work(),
        "stats",
    )(me, pos, cnt, *near(*kvs, *qds))


def grads_call(me, pos, cnt, stats, kvs, qds):
    return call(
        grads_kernel,
        MIXED + [struct((LINE * OWN, BLOCK, WIDE), F32), struct((LINE * OWN, BLOCK, WIDE), BF16)],
        [SMEM] * 3 + [VMEM] * (4 * LINE),
        scratch_lines()
        + [pltpu.VMEM((K_BLOCKS, BLOCK, WIDE), F32), pltpu.VMEM((Q_BLOCKS, BLOCK, WIDE), F32)]
        + [pltpu.VMEM((Q_BLOCKS, BLOCK), F32)] * 2
        + scratch_work(),
        "grads",
    )(me, pos, cnt, *near(*stats, *kvs, *qds))


def body(hits_in, w_query, w_key, w_value, w_out, grad_y, block_cell, cell_mask):
    rows = OWN * BLOCK
    ctx = lax.axis_index("ctx")
    y, x, core = ctx // (LINE * CORES), ctx // CORES % LINE, ctx % CORES
    me = jnp.stack([y, x, core]).astype(jnp.int32)
    pos, cnt = live_lists(block_cell, cell_mask, y, ctx % (LINE * CORES))

    wide = (HEADS, 2 * BLOCK, WIDE)
    given = (hits_in, w_key, w_value, w_query, grad_y, w_out)
    sent = call(
        project_kernel,
        struct(wide, BF16),
        [ANY] * 6,
        [pltpu.VMEM(g.shape, BF16) for g in given] + [pltpu.SemaphoreType.DMA((6,))],
        "project",
    )(*[pltpu.with_memory_space_constraint(g, pltpu.HBM) for g in given])
    got, pos, cnt, me = lax.optimization_barrier((exchange(sent), pos, cnt, me))
    kv = got[:, :BLOCK].reshape(rows, WIDE)
    qd = got[:, BLOCK:].reshape(rows, WIDE)
    kvs = [kv] + [ctx_shift(kv, dx=hop) for hop in HOPS[1:]]
    kvs = kvs + [ctx_shift(piece, dc=1) for piece in kvs]
    qds = [qd] + [ctx_shift(qd, dy=hop) for hop in HOPS[1:]]

    stats = stats_call(me, pos, cnt, kvs, qds)
    all_stats = [stats] + [ctx_shift(stats, dy=hop) for hop in HOPS[1:]]
    *y_parts, own, other = grads_call(me, pos, cnt, all_stats, kvs, qds)
    y_parts = [y_parts[0]] + [ctx_shift(p, dy=hop) for p, hop in zip(y_parts[1:], HOPS[1:])]
    other = ctx_shift(other, dc=1)
    x_parts = call(core_sum_kernel, MIXED, [SMEM, VMEM, VMEM], name="core_sum")(me, *near(own, other))
    x_parts = [x_parts[0]] + [ctx_shift(p, dx=hop) for p, hop in zip(x_parts[1:], HOPS[1:])]
    summed = call(line_sum_kernel, struct(wide, BF16), [VMEM] * (2 * LINE), name="line_sum")(
        *near(*x_parts, *y_parts)
    )
    full = struct(hits_in.shape, BF16)
    return call(output_kernel, (full, full), [VMEM] * 5, name="output")(
        *near(exchange(summed), w_query, w_key, w_value, w_out)
    )


def solution(mesh):
    row = P(("ctx", "head"), None)
    return jax.shard_map(
        body,
        mesh=mesh,
        in_specs=(row, P(), P(), P(), P(), row, P(), P()),
        out_specs=(row, row),
        check_vma=False,
    )
```

```python
import functools

import jax
import jax.numpy as jnp
from jax import lax
from jax.experimental import pallas as pl
from jax.experimental.pallas import tpu as pltpu
from jax.sharding import PartitionSpec as P

HEADS = 8
HEAD_DIM = 64
WIDE = 2 * HEAD_DIM
BLOCK = 128
KB_MAX = 21
SLOTS = 24
STATS_ITEM = 2
GRADS_ITEM = 4
STATS_UNROLL = 8
WHOLE_UNROLL = 6
HALF_UNROLL = 6
LINE = 4
CORES = 2
OWN = 8
Q_BLOCKS = LINE * OWN
K_BLOCKS = LINE * CORES * OWN
HOPS = (0, 1, -1, 2)
SCALE = HEAD_DIM ** (-0.5)
FAR = -1e30
F32 = jnp.float32
BF16 = jnp.bfloat16
VMEM_LIMIT = 32 * 1024 * 1024

VMEM = pl.BlockSpec(memory_space=pltpu.VMEM)
SMEM = pl.BlockSpec(memory_space=pltpu.SMEM)
ANY = pl.BlockSpec(memory_space=pl.ANY)
NT = (((1,), (1,)), ((), ()))
TN = (((0,), (0,)), ((), ()))


def call(kernel, out_shape, in_specs, scratch=(), name=None):
    return pl.pallas_call(
        kernel,
        out_shape=out_shape,
        in_specs=in_specs,
        out_specs=jax.tree.map(lambda _: VMEM, out_shape),
        scratch_shapes=scratch,
        compiler_params=pltpu.CompilerParams(vmem_limit_bytes=VMEM_LIMIT),
        name=name,
    )


def struct(shape, dtype):
    return jax.ShapeDtypeStruct(shape, dtype)


def near(*arrays):
    return [pltpu.with_memory_space_constraint(a, pltpu.VMEM) for a in arrays]


def project_kernel(*refs):
    out_ref, bufs, sems = refs[6], refs[7:13], refs[13]
    copies = [pltpu.make_async_copy(refs[i], bufs[i], sems.at[i]) for i in range(6)]
    for copy in copies:
        copy.start()

    def arrived(i):
        copies[i].wait()
        return bufs[i][...]

    x = arrived(0)
    k = jnp.dot(x, arrived(1), preferred_element_type=F32).astype(BF16)
    v = jnp.dot(x, arrived(2), preferred_element_type=F32).astype(BF16)
    q = jnp.dot(x, arrived(3), preferred_element_type=F32).astype(BF16)
    q = q * jnp.asarray(SCALE, BF16)
    gy = arrived(4)
    d = lax.dot_general(gy, arrived(5), NT, preferred_element_type=F32).astype(BF16)
    for h in range(HEADS):
        cols = slice(h * HEAD_DIM, (h + 1) * HEAD_DIM)
        out_ref[h, :BLOCK] = jnp.concatenate([k[:, cols], v[:, cols]], axis=1)
        out_ref[h, BLOCK:] = jnp.concatenate([q[:, cols], d[:, cols]], axis=1)


def line_of(hop, at):
    return (at - hop + LINE) % LINE


def load_lines(me_ref, kv_pieces, qd_pieces, kv_all, qd_all, sems):
    y, x, c = me_ref[0], me_ref[1], me_ref[2]
    copies = []
    rows = OWN * BLOCK
    for i, piece in enumerate(kv_pieces):
        hop, other = HOPS[i % LINE], i // LINE
        core = c if other == 0 else 1 - c
        at = pl.multiple_of((line_of(hop, x) * CORES + core) * rows, rows)
        copies.append(pltpu.make_async_copy(piece, kv_all.at[pl.ds(at, rows)], sems.at[i]))
    for i, piece in enumerate(qd_pieces):
        at = pl.multiple_of(line_of(HOPS[i], y) * rows, rows)
        copies.append(
            pltpu.make_async_copy(piece, qd_all.at[pl.ds(at, rows)], sems.at[len(kv_pieces) + i])
        )
    for copy in copies:
        copy.start()
    return copies


def query_pair(qd_all, b):
    qd = qd_all[pl.ds(pl.multiple_of(b * BLOCK, BLOCK), BLOCK), :]
    low = lax.broadcasted_iota(jnp.int32, qd.shape, 1) < HEAD_DIM
    zero = jnp.zeros_like(qd)
    return jnp.concatenate([jnp.where(low, qd, zero), jnp.where(low, zero, qd)], axis=0)


def build_items(cnt_ref, item_ref, size):
    def one(b, at):
        def put(j, at):
            item_ref[at] = b * 16 + j
            return at + 1

        return lax.fori_loop(0, (cnt_ref[b] + size - 1) // size, put, at)

    return lax.fori_loop(0, Q_BLOCKS, one, 0)


def build_halves(cnt_ref, whole_ref, half_ref):
    half = GRADS_ITEM // 2

    def one(b, at):
        wholes, halves = at
        left = cnt_ref[b] % GRADS_ITEM
        short = jnp.where((left > 0) & (left <= half), 1, 0)
        amount = (cnt_ref[b] + half - 1) // GRADS_ITEM

        def put(j, at):
            whole_ref[at] = b * 16 + j
            return at + 1

        wholes = lax.fori_loop(0, amount, put, wholes)
        half_ref[halves] = b * 16 + 2 * amount
        return wholes, halves + short

    return lax.fori_loop(0, Q_BLOCKS, one, (0, 0))


def read_item(item_ref, pos_ref, cnt_ref, at, amount, size):
    code = item_ref[jnp.minimum(at, amount - 1)]
    b, j = code // 16, code % 16
    limit = jnp.where(at < amount, cnt_ref[b], 0)
    places = [pos_ref[b, size * j + s] for s in range(size)]
    far = [jnp.where(size * j + s < limit, 0.0, FAR) for s in range(size)]
    return b, places, far


def item_products(kv_all, pair, places, far):
    kv = jnp.concatenate(
        [kv_all[pl.ds(pl.multiple_of(p * BLOCK, BLOCK), BLOCK), :] for p in places], axis=0
    )
    prod = lax.dot_general(kv, pair, NT, preferred_element_type=F32)
    scores = jnp.concatenate(
        [prod[s * BLOCK : (s + 1) * BLOCK, :BLOCK] + far[s] for s in range(len(places))], axis=0
    )
    return kv, scores, prod[:, BLOCK:]


def stats_kernel(me_ref, pos_ref, cnt_ref, *rest):
    kv_pieces, qd_pieces = rest[: 2 * LINE], rest[2 * LINE : 3 * LINE]
    out_ref, kv_all, qd_all, item_ref, sems = rest[3 * LINE :]
    copies = load_lines(me_ref, kv_pieces, qd_pieces, kv_all, qd_all, sems)
    out_ref[0] = jnp.full((Q_BLOCKS, BLOCK), FAR, F32)
    out_ref[1:] = jnp.zeros((2, Q_BLOCKS, BLOCK), F32)
    amount = build_items(cnt_ref, item_ref, STATS_ITEM)
    for copy in copies:
        copy.wait()

    def step(n, carry):
        done = []
        for u in range(STATS_UNROLL):
            at = n * STATS_UNROLL + u
            b, places, far = read_item(item_ref, pos_ref, cnt_ref, at, amount, STATS_ITEM)
            _, scores, dprobs = item_products(kv_all, query_pair(qd_all, b), places, far)
            top = jnp.max(scores, axis=0, keepdims=True)
            raw = jnp.exp(scores - top)
            total = jnp.sum(raw, axis=0, keepdims=True)
            dot = jnp.sum(raw * dprobs, axis=0, keepdims=True)
            done.append((pl.ds(b, 1), top, total, dot))
        for row, top, total, dot in done:
            old = out_ref[0, row, :]
            new = jnp.maximum(old, top)
            keep, take = jnp.exp(old - new), jnp.exp(top - new)
            out_ref[0, row, :] = new
            out_ref[1, row, :] = out_ref[1, row, :] * keep + total * take
            out_ref[2, row, :] = out_ref[2, row, :] * keep + dot * take
        return carry

    lax.fori_loop(0, (amount + STATS_UNROLL - 1) // STATS_UNROLL, step, 0)


def grads_kernel(me_ref, pos_ref, cnt_ref, *rest):
    stats, rest = rest[:LINE], rest[LINE:]
    kv_pieces, qd_pieces, rest = rest[: 2 * LINE], rest[2 * LINE : 3 * LINE], rest[3 * LINE :]
    y_refs, rest = rest[:LINE], rest[LINE:]
    own_ref, other_ref, kv_all, qd_all, key_ref, query_ref = rest[:6]
    lse_ref, delta_ref, whole_ref, half_ref, sems = rest[6:]
    copies = load_lines(me_ref, kv_pieces, qd_pieces, kv_all, qd_all, sems)

    top = functools.reduce(jnp.maximum, [s[0] for s in stats])
    weights = [jnp.exp(s[0] - top) for s in stats]
    total = sum(s[1] * w for s, w in zip(stats, weights))
    dot = sum(s[2] * w for s, w in zip(stats, weights))
    lse_ref[...] = top + jnp.log(total)
    delta_ref[...] = dot / total
    key_ref[...] = jnp.zeros_like(key_ref)
    query_ref[...] = jnp.zeros_like(query_ref)
    wholes, halves = build_halves(cnt_ref, whole_ref, half_ref)
    for copy in copies:
        copy.wait()

    def run(item_ref, amount, size, unroll):
        def step(n, carry):
            done = []
            for u in range(unroll):
                at = n * unroll + u
                b, places, far = read_item(item_ref, pos_ref, cnt_ref, at, amount, size)
                pair = query_pair(qd_all, b)
                kv, scores, dprobs = item_products(kv_all, pair, places, far)
                probs = jnp.exp(scores - lse_ref[pl.ds(b, 1), :])
                dscores = probs * (dprobs - delta_ref[pl.ds(b, 1), :])
                low = jnp.concatenate([dscores.astype(BF16), probs.astype(BF16)], axis=1)
                terms = jnp.dot(low, pair, preferred_element_type=F32)
                mixed = lax.dot_general(kv, low, TN, preferred_element_type=F32)
                out = jnp.concatenate([mixed[:HEAD_DIM, :BLOCK], mixed[HEAD_DIM:, BLOCK:]], axis=0)
                done.append((b, places, terms, out))
            for b, places, terms, out in done:
                for s, p in enumerate(places):
                    key_ref[p] = key_ref[p] + terms[s * BLOCK : (s + 1) * BLOCK]
                query_ref[b] = query_ref[b] + out
            return carry

        lax.fori_loop(0, (amount + unroll - 1) // unroll, step, 0)

    run(whole_ref, wholes, GRADS_ITEM, WHOLE_UNROLL)
    run(half_ref, halves, GRADS_ITEM // 2, HALF_UNROLL)
    y, core = me_ref[0], me_ref[2]

    def spread(n, carry):
        line, i = n // OWN, n % OWN
        own_ref[n] = key_ref[(line * CORES + core) * OWN + i]
        other_ref[n] = key_ref[(line * CORES + 1 - core) * OWN + i].astype(BF16)
        return carry

    lax.fori_loop(0, LINE * OWN, spread, 0)
    for k, hop in enumerate(HOPS):
        line = (y + hop + LINE) % LINE * OWN

        def scaled(i, carry):
            out = query_ref[line + i]
            out = jnp.concatenate([out[:HEAD_DIM] * SCALE, out[HEAD_DIM:]], axis=0)
            y_refs[k][i] = out.astype(y_refs[k].dtype)
            return carry

        lax.fori_loop(0, OWN, scaled, 0)


def core_sum_kernel(me_ref, own_ref, other_ref, *out_refs):
    x = me_ref[1]
    for k, hop in enumerate(HOPS):
        line = (x + hop + LINE) % LINE
        rows = pl.ds(line * OWN, OWN)
        out_refs[k][...] = (own_ref[rows] + other_ref[rows].astype(F32)).astype(out_refs[k].dtype)


def line_sum_kernel(*refs):
    xs, ys, out_ref = refs[:LINE], refs[LINE : 2 * LINE], refs[2 * LINE]
    for at, parts in ((0, xs), (BLOCK, ys)):
        out_ref[:, at : at + BLOCK] = sum(p[...].astype(F32) for p in parts).astype(BF16)


def output_kernel(in_ref, wq_ref, wk_ref, wv_ref, wo_ref, out_ref, grad_ref):
    gk = jnp.concatenate([in_ref[h, :BLOCK, :HEAD_DIM] for h in range(HEADS)], axis=1)
    gv = jnp.concatenate([in_ref[h, :BLOCK, HEAD_DIM:] for h in range(HEADS)], axis=1)
    gq = jnp.concatenate([in_ref[h, BLOCK : BLOCK + HEAD_DIM] for h in range(HEADS)], axis=0)
    att = jnp.concatenate([in_ref[h, BLOCK + HEAD_DIM :] for h in range(HEADS)], axis=0)
    out = lax.dot_general(att, wo_ref[...], TN, preferred_element_type=F32)
    out_ref[...] = out.astype(BF16)
    total = lax.dot_general(
        gq, wq_ref[...], (((0,), (1,)), ((), ())), preferred_element_type=F32
    )
    total = total + lax.dot_general(gk, wk_ref[...], NT, preferred_element_type=F32)
    total = total + lax.dot_general(gv, wv_ref[...], NT, preferred_element_type=F32)
    grad_ref[...] = total.astype(BF16)


def ctx_shift(x, dy=0, dx=0, dc=0):
    pairs = []
    for i in range(LINE * LINE * CORES):
        y, r, c = i // (LINE * CORES), i // CORES % LINE, i % CORES
        to = ((y + dy) % LINE * LINE + (r + dx) % LINE) * CORES + (c + dc) % CORES
        pairs.append((i, to))
    return lax.ppermute(x, "ctx", pairs)


def live_lists(block_cell, cell_mask, y, xc):
    cells = jnp.arange(cell_mask.shape[0], dtype=jnp.int32)
    by_line = block_cell.reshape(LINE, LINE * CORES, OWN)
    q_cell = lax.dynamic_index_in_dim(by_line, xc, 1, keepdims=False).reshape(Q_BLOCKS)
    k_cell = lax.dynamic_slice_in_dim(block_cell, y * K_BLOCKS, K_BLOCKS, 0)
    q_hot = (q_cell[:, None] == cells[None, :]).astype(BF16)
    k_hot = (k_cell[:, None] == cells[None, :]).astype(BF16)
    picked = jnp.dot(q_hot, cell_mask.astype(BF16), preferred_element_type=F32).astype(BF16)
    live = lax.dot_general(picked, k_hot, NT, preferred_element_type=F32)
    at = jnp.arange(K_BLOCKS, dtype=jnp.int32)
    upto = (at[:, None] <= at[None, :]).astype(BF16)
    rank = jnp.dot(live.astype(BF16), upto, preferred_element_type=F32)
    slots = jnp.arange(1, SLOTS + 1, dtype=jnp.int32).astype(F32)
    matched = (live[:, None, :] > 0.5) & (rank[:, None, :] == slots[None, :, None])
    pos = jnp.sum(jnp.where(matched, at[None, None, :], 0), axis=2)
    return pos, jnp.sum(live, axis=1).astype(jnp.int32)


def exchange(x):
    return lax.all_to_all(x, "head", split_axis=0, concat_axis=0, tiled=True)


def scratch_lines():
    return [
        pltpu.VMEM((K_BLOCKS * BLOCK, WIDE), BF16),
        pltpu.VMEM((Q_BLOCKS * BLOCK, WIDE), BF16),
    ]


def item_list(size):
    return pltpu.SMEM((Q_BLOCKS * SLOTS // size,), jnp.int32)


def piece_sems():
    return pltpu.SemaphoreType.DMA((3 * LINE,))


MIXED = [struct((OWN, BLOCK, WIDE), F32)] + [struct((OWN, BLOCK, WIDE), BF16)] * (LINE - 1)


def stats_call(me, pos, cnt, kvs, qds):
    return call(
        stats_kernel,
        struct((3, Q_BLOCKS, BLOCK), F32),
        [SMEM] * 3 + [VMEM] * (3 * LINE),
        scratch_lines() + [item_list(STATS_ITEM), piece_sems()],
        "stats",
    )(me, pos, cnt, *near(*kvs, *qds))


def grads_call(me, pos, cnt, stats, kvs, qds):
    return call(
        grads_kernel,
        MIXED + [struct((LINE * OWN, BLOCK, WIDE), F32), struct((LINE * OWN, BLOCK, WIDE), BF16)],
        [SMEM] * 3 + [VMEM] * (4 * LINE),
        scratch_lines()
        + [pltpu.VMEM((K_BLOCKS, BLOCK, WIDE), F32), pltpu.VMEM((Q_BLOCKS, BLOCK, WIDE), F32)]
        + [pltpu.VMEM((Q_BLOCKS, BLOCK), F32)] * 2
        + [item_list(GRADS_ITEM), pltpu.SMEM((Q_BLOCKS,), jnp.int32), piece_sems()],
        "grads",
    )(me, pos, cnt, *near(*stats, *kvs, *qds))


def body(hits_in, w_query, w_key, w_value, w_out, grad_y, block_cell, cell_mask):
    rows = OWN * BLOCK
    ctx = lax.axis_index("ctx")
    y, x, core = ctx // (LINE * CORES), ctx // CORES % LINE, ctx % CORES
    me = jnp.stack([y, x, core]).astype(jnp.int32)
    pos, cnt = live_lists(block_cell, cell_mask, y, ctx % (LINE * CORES))

    wide = (HEADS, 2 * BLOCK, WIDE)
    given = (hits_in, w_key, w_value, w_query, grad_y, w_out)
    sent = call(
        project_kernel,
        struct(wide, BF16),
        [ANY] * 6,
        [pltpu.VMEM(g.shape, BF16) for g in given] + [pltpu.SemaphoreType.DMA((6,))],
        "project",
    )(*[pltpu.with_memory_space_constraint(g, pltpu.HBM) for g in given])
    got, pos, cnt, me = lax.optimization_barrier((exchange(sent), pos, cnt, me))
    kv = got[:, :BLOCK].reshape(rows, WIDE)
    qd = got[:, BLOCK:].reshape(rows, WIDE)
    kvs = [kv] + [ctx_shift(kv, dx=hop) for hop in HOPS[1:]]
    other = ctx_shift(kv, dc=1)
    qd, other = lax.optimization_barrier((qd, other))
    kvs = kvs + [other] + [ctx_shift(piece, dc=1) for piece in kvs[1:]]
    qds = [qd] + [ctx_shift(qd, dy=hop) for hop in HOPS[1:]]

    stats = stats_call(me, pos, cnt, kvs, qds)
    all_stats = [stats] + [ctx_shift(stats, dy=hop) for hop in HOPS[1:]]
    *y_parts, own, other = grads_call(me, pos, cnt, all_stats, kvs, qds)
    y_parts = [y_parts[0]] + [ctx_shift(p, dy=hop) for p, hop in zip(y_parts[1:], HOPS[1:])]
    other = ctx_shift(other, dc=1)
    x_parts = call(core_sum_kernel, MIXED, [SMEM, VMEM, VMEM], name="core_sum")(me, *near(own, other))
    x_parts = [x_parts[0]] + [ctx_shift(p, dx=hop) for p, hop in zip(x_parts[1:], HOPS[1:])]
    summed = call(line_sum_kernel, struct(wide, BF16), [VMEM] * (2 * LINE), name="line_sum")(
        *near(*x_parts, *y_parts)
    )
    full = struct(hits_in.shape, BF16)
    return call(output_kernel, (full, full), [VMEM] * 5, name="output")(
        *near(exchange(summed), w_query, w_key, w_value, w_out)
    )


def solution(mesh):
    row = P(("ctx", "head"), None)
    return jax.shard_map(
        body,
        mesh=mesh,
        in_specs=(row, P(), P(), P(), P(), row, P(), P()),
        out_specs=(row, row),
        check_vma=False,
    )
```

```python
import functools

import jax
import jax.numpy as jnp
from jax import lax
from jax.experimental import pallas as pl
from jax.experimental.pallas import tpu as pltpu
from jax.sharding import PartitionSpec as P

HEADS = 8
HEAD_DIM = 64
WIDE = 2 * HEAD_DIM
BLOCK = 128
KB_MAX = 21
SLOTS = 24
STATS_MOST = 11
GRADS_MOST = 6
STATS_ITEM = 2
GRADS_ITEM = 4
STATS_UNROLL = 8
WHOLE_UNROLL = 6
HALF_UNROLL = 6
LINE = 4
CORES = 2
OWN = 8
Q_BLOCKS = LINE * OWN
K_BLOCKS = LINE * CORES * OWN
HOPS = (0, 1, -1, 2)
SCALE = HEAD_DIM ** (-0.5)
FAR = -1e30
F32 = jnp.float32
BF16 = jnp.bfloat16
VMEM_LIMIT = 32 * 1024 * 1024

VMEM = pl.BlockSpec(memory_space=pltpu.VMEM)
SMEM = pl.BlockSpec(memory_space=pltpu.SMEM)
ANY = pl.BlockSpec(memory_space=pl.ANY)
NT = (((1,), (1,)), ((), ()))
TN = (((0,), (0,)), ((), ()))


def call(kernel, out_shape, in_specs, scratch=(), name=None):
    return pl.pallas_call(
        kernel,
        out_shape=out_shape,
        in_specs=in_specs,
        out_specs=jax.tree.map(lambda _: VMEM, out_shape),
        scratch_shapes=scratch,
        compiler_params=pltpu.CompilerParams(vmem_limit_bytes=VMEM_LIMIT),
        name=name,
    )


def struct(shape, dtype):
    return jax.ShapeDtypeStruct(shape, dtype)


def near(*arrays):
    return [pltpu.with_memory_space_constraint(a, pltpu.VMEM) for a in arrays]


def project_kernel(*refs):
    out_ref, bufs, sems = refs[6], refs[7:13], refs[13]
    copies = [pltpu.make_async_copy(refs[i], bufs[i], sems.at[i]) for i in range(6)]
    for copy in copies:
        copy.start()

    def arrived(i):
        copies[i].wait()
        return bufs[i][...]

    x = arrived(0)
    k = jnp.dot(x, arrived(1), preferred_element_type=F32).astype(BF16)
    v = jnp.dot(x, arrived(2), preferred_element_type=F32).astype(BF16)
    q = jnp.dot(x, arrived(3), preferred_element_type=F32).astype(BF16)
    q = q * jnp.asarray(SCALE, BF16)
    gy = arrived(4)
    d = lax.dot_general(gy, arrived(5), NT, preferred_element_type=F32).astype(BF16)
    for h in range(HEADS):
        cols = slice(h * HEAD_DIM, (h + 1) * HEAD_DIM)
        out_ref[h, :BLOCK] = jnp.concatenate([k[:, cols], v[:, cols]], axis=1)
        out_ref[h, BLOCK:] = jnp.concatenate([q[:, cols], d[:, cols]], axis=1)


def line_of(hop, at):
    return (at - hop + LINE) % LINE


def load_lines(me_ref, kv_pieces, qd_pieces, kv_all, qd_all, sems):
    y, x, c = me_ref[0], me_ref[1], me_ref[2]
    copies = []
    rows = OWN * BLOCK
    for i, piece in enumerate(kv_pieces):
        hop, other = HOPS[i % LINE], i // LINE
        core = c if other == 0 else 1 - c
        at = pl.multiple_of((line_of(hop, x) * CORES + core) * rows, rows)
        copies.append(pltpu.make_async_copy(piece, kv_all.at[pl.ds(at, rows)], sems.at[i]))
    for i, piece in enumerate(qd_pieces):
        at = pl.multiple_of(line_of(HOPS[i], y) * rows, rows)
        copies.append(
            pltpu.make_async_copy(piece, qd_all.at[pl.ds(at, rows)], sems.at[len(kv_pieces) + i])
        )
    for copy in copies:
        copy.start()
    return copies


def query_pair(qd_all, b):
    qd = qd_all[pl.ds(pl.multiple_of(b * BLOCK, BLOCK), BLOCK), :]
    low = lax.broadcasted_iota(jnp.int32, qd.shape, 1) < HEAD_DIM
    zero = jnp.zeros_like(qd)
    return jnp.concatenate([jnp.where(low, qd, zero), jnp.where(low, zero, qd)], axis=0)


def read_item(item_ref, base, pos_ref, cnt_ref, at, amount, size):
    code = item_ref[base + jnp.minimum(at, amount - 1)]
    b, j = code // 16, code % 16
    limit = jnp.where(at < amount, cnt_ref[b], 0)
    places = [pos_ref[b, size * j + s] for s in range(size)]
    far = [jnp.where(size * j + s < limit, 0.0, FAR) for s in range(size)]
    return b, places, far


def item_products(kv_all, pair, places, far):
    kv = jnp.concatenate(
        [kv_all[pl.ds(pl.multiple_of(p * BLOCK, BLOCK), BLOCK), :] for p in places], axis=0
    )
    prod = lax.dot_general(kv, pair, NT, preferred_element_type=F32)
    scores = jnp.concatenate(
        [prod[s * BLOCK : (s + 1) * BLOCK, :BLOCK] + far[s] for s in range(len(places))], axis=0
    )
    return kv, scores, prod[:, BLOCK:]


def stats_kernel(me_ref, pos_ref, cnt_ref, item_ref, *rest):
    kv_pieces, qd_pieces = rest[: 2 * LINE], rest[2 * LINE : 3 * LINE]
    out_ref, kv_all, qd_all, sems = rest[3 * LINE :]
    copies = load_lines(me_ref, kv_pieces, qd_pieces, kv_all, qd_all, sems)
    out_ref[0] = jnp.full((Q_BLOCKS, BLOCK), FAR, F32)
    out_ref[1:] = jnp.zeros((2, Q_BLOCKS, BLOCK), F32)
    amount = item_ref[Q_BLOCKS * STATS_MOST]
    for copy in copies:
        copy.wait()

    def step(n, carry):
        done = []
        for u in range(STATS_UNROLL):
            at = n * STATS_UNROLL + u
            b, places, far = read_item(item_ref, 0, pos_ref, cnt_ref, at, amount, STATS_ITEM)
            _, scores, dprobs = item_products(kv_all, query_pair(qd_all, b), places, far)
            top = jnp.max(scores, axis=0, keepdims=True)
            raw = jnp.exp(scores - top)
            total = jnp.sum(raw, axis=0, keepdims=True)
            dot = jnp.sum(raw * dprobs, axis=0, keepdims=True)
            done.append((pl.ds(b, 1), top, total, dot))
        for row, top, total, dot in done:
            old = out_ref[0, row, :]
            new = jnp.maximum(old, top)
            keep, take = jnp.exp(old - new), jnp.exp(top - new)
            out_ref[0, row, :] = new
            out_ref[1, row, :] = out_ref[1, row, :] * keep + total * take
            out_ref[2, row, :] = out_ref[2, row, :] * keep + dot * take
        return carry

    lax.fori_loop(0, (amount + STATS_UNROLL - 1) // STATS_UNROLL, step, 0)


def grads_kernel(me_ref, pos_ref, cnt_ref, item_ref, *rest):
    stats, rest = rest[:LINE], rest[LINE:]
    kv_pieces, qd_pieces, rest = rest[: 2 * LINE], rest[2 * LINE : 3 * LINE], rest[3 * LINE :]
    y_refs, rest = rest[:LINE], rest[LINE:]
    own_ref, other_ref, kv_all, qd_all, key_ref, query_ref = rest[:6]
    lse_ref, delta_ref, sems = rest[6:]
    copies = load_lines(me_ref, kv_pieces, qd_pieces, kv_all, qd_all, sems)

    top = functools.reduce(jnp.maximum, [s[0] for s in stats])
    weights = [jnp.exp(s[0] - top) for s in stats]
    total = sum(s[1] * w for s, w in zip(stats, weights))
    dot = sum(s[2] * w for s, w in zip(stats, weights))
    lse_ref[...] = top + jnp.log(total)
    delta_ref[...] = dot / total
    key_ref[...] = jnp.zeros_like(key_ref)
    query_ref[...] = jnp.zeros_like(query_ref)
    whole_end = Q_BLOCKS * GRADS_MOST
    half_end = whole_end + 1 + Q_BLOCKS
    for copy in copies:
        copy.wait()

    def run(base, amount, size, unroll):
        def step(n, carry):
            done = []
            for u in range(unroll):
                at = n * unroll + u
                b, places, far = read_item(item_ref, base, pos_ref, cnt_ref, at, amount, size)
                pair = query_pair(qd_all, b)
                kv, scores, dprobs = item_products(kv_all, pair, places, far)
                probs = jnp.exp(scores - lse_ref[pl.ds(b, 1), :])
                dscores = probs * (dprobs - delta_ref[pl.ds(b, 1), :])
                low = jnp.concatenate([dscores.astype(BF16), probs.astype(BF16)], axis=1)
                terms = jnp.dot(low, pair, preferred_element_type=F32)
                mixed = lax.dot_general(kv, low, TN, preferred_element_type=F32)
                out = jnp.concatenate([mixed[:HEAD_DIM, :BLOCK], mixed[HEAD_DIM:, BLOCK:]], axis=0)
                done.append((b, places, terms, out))
            for b, places, terms, out in done:
                for s, p in enumerate(places):
                    key_ref[p] = key_ref[p] + terms[s * BLOCK : (s + 1) * BLOCK]
                query_ref[b] = query_ref[b] + out
            return carry

        lax.fori_loop(0, (amount + unroll - 1) // unroll, step, 0)

    run(0, item_ref[whole_end], GRADS_ITEM, WHOLE_UNROLL)
    run(whole_end + 1, item_ref[half_end], GRADS_ITEM // 2, HALF_UNROLL)
    y, core = me_ref[0], me_ref[2]

    def spread(n, carry):
        line, i = n // OWN, n % OWN
        own_ref[n] = key_ref[(line * CORES + core) * OWN + i]
        other_ref[n] = key_ref[(line * CORES + 1 - core) * OWN + i].astype(BF16)
        return carry

    lax.fori_loop(0, LINE * OWN, spread, 0)
    for k, hop in enumerate(HOPS):
        line = (y + hop + LINE) % LINE * OWN

        def scaled(i, carry):
            out = query_ref[line + i]
            out = jnp.concatenate([out[:HEAD_DIM] * SCALE, out[HEAD_DIM:]], axis=0)
            y_refs[k][i] = out.astype(y_refs[k].dtype)
            return carry

        lax.fori_loop(0, OWN, scaled, 0)


def core_sum_kernel(me_ref, own_ref, other_ref, *out_refs):
    x = me_ref[1]
    for k, hop in enumerate(HOPS):
        line = (x + hop + LINE) % LINE
        rows = pl.ds(line * OWN, OWN)
        out_refs[k][...] = (own_ref[rows] + other_ref[rows].astype(F32)).astype(out_refs[k].dtype)


def line_sum_kernel(*refs):
    xs, ys, out_ref = refs[:LINE], refs[LINE : 2 * LINE], refs[2 * LINE]
    for at, parts in ((0, xs), (BLOCK, ys)):
        out_ref[:, at : at + BLOCK] = sum(p[...].astype(F32) for p in parts).astype(BF16)


def output_kernel(in_ref, wq_ref, wk_ref, wv_ref, wo_ref, out_ref, grad_ref):
    gk = jnp.concatenate([in_ref[h, :BLOCK, :HEAD_DIM] for h in range(HEADS)], axis=1)
    gv = jnp.concatenate([in_ref[h, :BLOCK, HEAD_DIM:] for h in range(HEADS)], axis=1)
    gq = jnp.concatenate([in_ref[h, BLOCK : BLOCK + HEAD_DIM] for h in range(HEADS)], axis=0)
    att = jnp.concatenate([in_ref[h, BLOCK + HEAD_DIM :] for h in range(HEADS)], axis=0)
    out = lax.dot_general(att, wo_ref[...], TN, preferred_element_type=F32)
    out_ref[...] = out.astype(BF16)
    total = lax.dot_general(
        gq, wq_ref[...], (((0,), (1,)), ((), ())), preferred_element_type=F32
    )
    total = total + lax.dot_general(gk, wk_ref[...], NT, preferred_element_type=F32)
    total = total + lax.dot_general(gv, wv_ref[...], NT, preferred_element_type=F32)
    grad_ref[...] = total.astype(BF16)


def ctx_shift(x, dy=0, dx=0, dc=0):
    pairs = []
    for i in range(LINE * LINE * CORES):
        y, r, c = i // (LINE * CORES), i // CORES % LINE, i % CORES
        to = ((y + dy) % LINE * LINE + (r + dx) % LINE) * CORES + (c + dc) % CORES
        pairs.append((i, to))
    return lax.ppermute(x, "ctx", pairs)


def live_lists(block_cell, cell_mask, y, xc):
    cells = jnp.arange(cell_mask.shape[0], dtype=jnp.int32)
    by_line = block_cell.reshape(LINE, LINE * CORES, OWN)
    q_cell = lax.dynamic_index_in_dim(by_line, xc, 1, keepdims=False).reshape(Q_BLOCKS)
    k_cell = lax.dynamic_slice_in_dim(block_cell, y * K_BLOCKS, K_BLOCKS, 0)
    q_hot = (q_cell[:, None] == cells[None, :]).astype(BF16)
    k_hot = (k_cell[:, None] == cells[None, :]).astype(BF16)
    picked = jnp.dot(q_hot, cell_mask.astype(BF16), preferred_element_type=F32).astype(BF16)
    live = lax.dot_general(picked, k_hot, NT, preferred_element_type=F32)
    at = jnp.arange(K_BLOCKS, dtype=jnp.int32)
    upto = (at[:, None] <= at[None, :]).astype(BF16)
    rank = jnp.dot(live.astype(BF16), upto, preferred_element_type=F32)
    slots = jnp.arange(1, SLOTS + 1, dtype=jnp.int32).astype(F32)
    matched = (live[:, None, :] > 0.5) & (rank[:, None, :] == slots[None, :, None])
    pos = jnp.sum(jnp.where(matched, at[None, None, :], 0), axis=2)
    return pos, jnp.sum(live, axis=1).astype(jnp.int32)


def item_table(amounts, first, most):
    b = jnp.arange(Q_BLOCKS, dtype=jnp.int32)
    j = jnp.arange(most, dtype=jnp.int32)
    start = jnp.sum(jnp.where(b[None, :] < b[:, None], amounts[None, :], 0), axis=1)
    at = jnp.where(j[None, :] < amounts[:, None], start[:, None] + j[None, :], -1)
    code = (b * 16 + first)[:, None] + j[None, :]
    slot = jnp.arange(Q_BLOCKS * most, dtype=jnp.int32)
    hit = at[None] == slot[:, None, None]
    return jnp.sum(jnp.where(hit, code[None], 0), axis=(1, 2)), jnp.sum(amounts)[None]


def item_tables(cnt):
    half = GRADS_ITEM // 2
    none = jnp.zeros_like(cnt)
    whole = (cnt + half - 1) // GRADS_ITEM
    left = cnt % GRADS_ITEM
    short = ((left > 0) & (left <= half)).astype(jnp.int32)
    stats = item_table((cnt + STATS_ITEM - 1) // STATS_ITEM, none, STATS_MOST)
    wholes = item_table(whole, none, GRADS_MOST)
    halves = item_table(short, 2 * whole, 1)
    return jnp.concatenate(stats), jnp.concatenate(wholes + halves)


def exchange(x):
    return lax.all_to_all(x, "head", split_axis=0, concat_axis=0, tiled=True)


def scratch_lines():
    return [
        pltpu.VMEM((K_BLOCKS * BLOCK, WIDE), BF16),
        pltpu.VMEM((Q_BLOCKS * BLOCK, WIDE), BF16),
    ]


def piece_sems():
    return pltpu.SemaphoreType.DMA((3 * LINE,))


MIXED = [struct((OWN, BLOCK, WIDE), F32)] + [struct((OWN, BLOCK, WIDE), BF16)] * (LINE - 1)


def stats_call(lists, kvs, qds):
    return call(
        stats_kernel,
        struct((3, Q_BLOCKS, BLOCK), F32),
        [SMEM] * 4 + [VMEM] * (3 * LINE),
        scratch_lines() + [piece_sems()],
        "stats",
    )(*lists, *near(*kvs, *qds))


def grads_call(lists, stats, kvs, qds):
    return call(
        grads_kernel,
        MIXED + [struct((LINE * OWN, BLOCK, WIDE), F32), struct((LINE * OWN, BLOCK, WIDE), BF16)],
        [SMEM] * 4 + [VMEM] * (4 * LINE),
        scratch_lines()
        + [pltpu.VMEM((K_BLOCKS, BLOCK, WIDE), F32), pltpu.VMEM((Q_BLOCKS, BLOCK, WIDE), F32)]
        + [pltpu.VMEM((Q_BLOCKS, BLOCK), F32)] * 2
        + [piece_sems()],
        "grads",
    )(*lists, *near(*stats, *kvs, *qds))


def body(hits_in, w_query, w_key, w_value, w_out, grad_y, block_cell, cell_mask):
    rows = OWN * BLOCK
    ctx = lax.axis_index("ctx")
    y, x, core = ctx // (LINE * CORES), ctx // CORES % LINE, ctx % CORES
    me = jnp.stack([y, x, core]).astype(jnp.int32)
    pos, cnt = live_lists(block_cell, cell_mask, y, ctx % (LINE * CORES))

    wide = (HEADS, 2 * BLOCK, WIDE)
    given = (hits_in, w_key, w_value, w_query, grad_y, w_out)
    sent = call(
        project_kernel,
        struct(wide, BF16),
        [ANY] * 6,
        [pltpu.VMEM(g.shape, BF16) for g in given] + [pltpu.SemaphoreType.DMA((6,))],
        "project",
    )(*[pltpu.with_memory_space_constraint(g, pltpu.HBM) for g in given])
    tables = item_tables(cnt)
    got, me, pos, cnt, tables = lax.optimization_barrier((exchange(sent), me, pos, cnt, tables))
    kv = got[:, :BLOCK].reshape(rows, WIDE)
    qd = got[:, BLOCK:].reshape(rows, WIDE)
    kvs = [kv] + [ctx_shift(kv, dx=hop) for hop in HOPS[1:]]
    other = ctx_shift(kv, dc=1)
    qd, other = lax.optimization_barrier((qd, other))
    kvs = kvs + [other] + [ctx_shift(piece, dc=1) for piece in kvs[1:]]
    qds = [qd] + [ctx_shift(qd, dy=hop) for hop in HOPS[1:]]

    stats = stats_call((me, pos, cnt, tables[0]), kvs, qds)
    all_stats = [stats] + [ctx_shift(stats, dy=hop) for hop in HOPS[1:]]
    *y_parts, own, other = grads_call((me, pos, cnt, tables[1]), all_stats, kvs, qds)
    y_parts = [y_parts[0]] + [ctx_shift(p, dy=hop) for p, hop in zip(y_parts[1:], HOPS[1:])]
    other = ctx_shift(other, dc=1)
    x_parts = call(core_sum_kernel, MIXED, [SMEM, VMEM, VMEM], name="core_sum")(me, *near(own, other))
    x_parts = [x_parts[0]] + [ctx_shift(p, dx=hop) for p, hop in zip(x_parts[1:], HOPS[1:])]
    summed = call(line_sum_kernel, struct(wide, BF16), [VMEM] * (2 * LINE), name="line_sum")(
        *near(*x_parts, *y_parts)
    )
    full = struct(hits_in.shape, BF16)
    return call(output_kernel, (full, full), [VMEM] * 5, name="output")(
        *near(exchange(summed), w_query, w_key, w_value, w_out)
    )


def solution(mesh):
    row = P(("ctx", "head"), None)
    return jax.shard_map(
        body,
        mesh=mesh,
        in_specs=(row, P(), P(), P(), P(), row, P(), P()),
        out_specs=(row, row),
        check_vma=False,
    )
```

```python
import functools

import jax
import jax.numpy as jnp
from jax import lax
from jax.experimental import pallas as pl
from jax.experimental.pallas import tpu as pltpu
from jax.sharding import PartitionSpec as P

HEADS = 8
HEAD_DIM = 64
WIDE = 2 * HEAD_DIM
BLOCK = 128
KB_MAX = 21
SLOTS = 24
STATS_MOST = 11
GRADS_MOST = 6
STATS_ITEM = 2
GRADS_ITEM = 4
STATS_UNROLL = 8
WHOLE_UNROLL = 6
HALF_UNROLL = 6
LINE = 4
CORES = 2
OWN = 8
Q_BLOCKS = LINE * OWN
K_BLOCKS = LINE * CORES * OWN
HOPS = (0, 1, -1, 2)
SCALE = HEAD_DIM ** (-0.5)
FAR = -1e30
F32 = jnp.float32
BF16 = jnp.bfloat16
VMEM_LIMIT = 32 * 1024 * 1024

VMEM = pl.BlockSpec(memory_space=pltpu.VMEM)
SMEM = pl.BlockSpec(memory_space=pltpu.SMEM)
ANY = pl.BlockSpec(memory_space=pl.ANY)
NT = (((1,), (1,)), ((), ()))
TN = (((0,), (0,)), ((), ()))


def call(kernel, out_shape, in_specs, scratch=(), name=None):
    return pl.pallas_call(
        kernel,
        out_shape=out_shape,
        in_specs=in_specs,
        out_specs=jax.tree.map(lambda _: VMEM, out_shape),
        scratch_shapes=scratch,
        compiler_params=pltpu.CompilerParams(vmem_limit_bytes=VMEM_LIMIT),
        name=name,
    )


def struct(shape, dtype):
    return jax.ShapeDtypeStruct(shape, dtype)


def near(*arrays):
    return [pltpu.with_memory_space_constraint(a, pltpu.VMEM) for a in arrays]


def project_kernel(*refs):
    out_ref, bufs, sems = refs[6], refs[7:13], refs[13]
    copies = [pltpu.make_async_copy(refs[i], bufs[i], sems.at[i]) for i in range(6)]
    for copy in copies:
        copy.start()

    def arrived(i):
        copies[i].wait()
        return bufs[i][...]

    x = arrived(0)
    k = jnp.dot(x, arrived(1), preferred_element_type=F32).astype(BF16)
    v = jnp.dot(x, arrived(2), preferred_element_type=F32).astype(BF16)
    q = jnp.dot(x, arrived(3), preferred_element_type=F32).astype(BF16)
    q = q * jnp.asarray(SCALE, BF16)
    gy = arrived(4)
    d = lax.dot_general(gy, arrived(5), NT, preferred_element_type=F32).astype(BF16)
    for h in range(HEADS):
        cols = slice(h * HEAD_DIM, (h + 1) * HEAD_DIM)
        out_ref[h, :BLOCK] = jnp.concatenate([k[:, cols], v[:, cols]], axis=1)
        out_ref[h, BLOCK:] = jnp.concatenate([q[:, cols], d[:, cols]], axis=1)


def line_of(hop, at):
    return (at - hop + LINE) % LINE


def load_lines(me_ref, kv_pieces, qd_pieces, kv_all, qd_all, sems):
    y, x, c = me_ref[0], me_ref[1], me_ref[2]
    copies = []
    rows = OWN * BLOCK
    for i, piece in enumerate(kv_pieces):
        hop, other = HOPS[i % LINE], i // LINE
        core = c if other == 0 else 1 - c
        at = pl.multiple_of((line_of(hop, x) * CORES + core) * rows, rows)
        copies.append(pltpu.make_async_copy(piece, kv_all.at[pl.ds(at, rows)], sems.at[i]))
    for i, piece in enumerate(qd_pieces):
        at = pl.multiple_of(line_of(HOPS[i], y) * rows, rows)
        copies.append(
            pltpu.make_async_copy(piece, qd_all.at[pl.ds(at, rows)], sems.at[len(kv_pieces) + i])
        )
    for copy in copies:
        copy.start()
    return copies


def query_pair(qd_all, b):
    qd = qd_all[pl.ds(pl.multiple_of(b * BLOCK, BLOCK), BLOCK), :]
    low = lax.broadcasted_iota(jnp.int32, qd.shape, 1) < HEAD_DIM
    zero = jnp.zeros_like(qd)
    return jnp.concatenate([jnp.where(low, qd, zero), jnp.where(low, zero, qd)], axis=0)


def read_item(item_ref, base, pos_ref, cnt_ref, at, amount, size):
    code = item_ref[base + jnp.minimum(at, amount - 1)]
    b, j = code // 16, code % 16
    limit = jnp.where(at < amount, cnt_ref[b], 0)
    places = [pos_ref[b, size * j + s] for s in range(size)]
    far = [jnp.where(size * j + s < limit, 0.0, FAR) for s in range(size)]
    return b, places, far


def item_products(kv_all, pair, places, far):
    kv = jnp.concatenate(
        [kv_all[pl.ds(pl.multiple_of(p * BLOCK, BLOCK), BLOCK), :] for p in places], axis=0
    )
    prod = lax.dot_general(kv, pair, NT, preferred_element_type=F32)
    scores = jnp.concatenate(
        [prod[s * BLOCK : (s + 1) * BLOCK, :BLOCK] + far[s] for s in range(len(places))], axis=0
    )
    return kv, scores, prod[:, BLOCK:]


def stats_kernel(me_ref, pos_ref, cnt_ref, item_ref, *rest):
    kv_pieces, qd_pieces = rest[: 2 * LINE], rest[2 * LINE : 3 * LINE]
    out_ref, kv_all, qd_all, sems = rest[3 * LINE :]
    copies = load_lines(me_ref, kv_pieces, qd_pieces, kv_all, qd_all, sems)
    out_ref[0] = jnp.full((Q_BLOCKS, BLOCK), FAR, F32)
    out_ref[1:] = jnp.zeros((2, Q_BLOCKS, BLOCK), F32)
    amount = item_ref[Q_BLOCKS * STATS_MOST]
    for copy in copies:
        copy.wait()

    def step(n, carry):
        done = []
        for u in range(STATS_UNROLL):
            at = n * STATS_UNROLL + u
            b, places, far = read_item(item_ref, 0, pos_ref, cnt_ref, at, amount, STATS_ITEM)
            _, scores, dprobs = item_products(kv_all, query_pair(qd_all, b), places, far)
            top = jnp.max(scores, axis=0, keepdims=True)
            raw = jnp.exp(scores - top)
            total = jnp.sum(raw, axis=0, keepdims=True)
            dot = jnp.sum(raw * dprobs, axis=0, keepdims=True)
            done.append((pl.ds(b, 1), top, total, dot))
        for row, top, total, dot in done:
            old = out_ref[0, row, :]
            new = jnp.maximum(old, top)
            keep, take = jnp.exp(old - new), jnp.exp(top - new)
            out_ref[0, row, :] = new
            out_ref[1, row, :] = out_ref[1, row, :] * keep + total * take
            out_ref[2, row, :] = out_ref[2, row, :] * keep + dot * take
        return carry

    lax.fori_loop(0, (amount + STATS_UNROLL - 1) // STATS_UNROLL, step, 0)


def grads_kernel(me_ref, pos_ref, cnt_ref, item_ref, *rest):
    stats, rest = rest[:LINE], rest[LINE:]
    kv_all, qd_all, rest = rest[0], rest[1], rest[2:]
    y_refs, rest = rest[:LINE], rest[LINE:]
    own_ref, other_ref, key_ref, query_ref, lse_ref, delta_ref = rest

    top = functools.reduce(jnp.maximum, [s[0] for s in stats])
    weights = [jnp.exp(s[0] - top) for s in stats]
    total = sum(s[1] * w for s, w in zip(stats, weights))
    dot = sum(s[2] * w for s, w in zip(stats, weights))
    lse_ref[...] = top + jnp.log(total)
    delta_ref[...] = dot / total
    key_ref[...] = jnp.zeros_like(key_ref)
    query_ref[...] = jnp.zeros_like(query_ref)
    whole_end = Q_BLOCKS * GRADS_MOST
    half_end = whole_end + 1 + Q_BLOCKS

    def run(base, amount, size, unroll):
        def step(n, carry):
            done = []
            for u in range(unroll):
                at = n * unroll + u
                b, places, far = read_item(item_ref, base, pos_ref, cnt_ref, at, amount, size)
                pair = query_pair(qd_all, b)
                kv, scores, dprobs = item_products(kv_all, pair, places, far)
                probs = jnp.exp(scores - lse_ref[pl.ds(b, 1), :])
                dscores = probs * (dprobs - delta_ref[pl.ds(b, 1), :])
                low = jnp.concatenate([dscores.astype(BF16), probs.astype(BF16)], axis=1)
                terms = jnp.dot(low, pair, preferred_element_type=F32)
                mixed = lax.dot_general(kv, low, TN, preferred_element_type=F32)
                out = jnp.concatenate([mixed[:HEAD_DIM, :BLOCK], mixed[HEAD_DIM:, BLOCK:]], axis=0)
                done.append((b, places, terms, out))
            for b, places, terms, out in done:
                for s, p in enumerate(places):
                    key_ref[p] = key_ref[p] + terms[s * BLOCK : (s + 1) * BLOCK]
                query_ref[b] = query_ref[b] + out
            return carry

        lax.fori_loop(0, (amount + unroll - 1) // unroll, step, 0)

    run(0, item_ref[whole_end], GRADS_ITEM, WHOLE_UNROLL)
    run(whole_end + 1, item_ref[half_end], GRADS_ITEM // 2, HALF_UNROLL)
    y, core = me_ref[0], me_ref[2]

    def spread(n, carry):
        line, i = n // OWN, n % OWN
        own_ref[n] = key_ref[(line * CORES + core) * OWN + i]
        other_ref[n] = key_ref[(line * CORES + 1 - core) * OWN + i].astype(BF16)
        return carry

    lax.fori_loop(0, LINE * OWN, spread, 0)
    for k, hop in enumerate(HOPS):
        line = (y + hop + LINE) % LINE * OWN

        def scaled(i, carry):
            out = query_ref[line + i]
            out = jnp.concatenate([out[:HEAD_DIM] * SCALE, out[HEAD_DIM:]], axis=0)
            y_refs[k][i] = out.astype(y_refs[k].dtype)
            return carry

        lax.fori_loop(0, OWN, scaled, 0)


def core_sum_kernel(me_ref, own_ref, other_ref, *out_refs):
    x = me_ref[1]
    for k, hop in enumerate(HOPS):
        line = (x + hop + LINE) % LINE
        rows = pl.ds(line * OWN, OWN)
        out_refs[k][...] = (own_ref[rows] + other_ref[rows].astype(F32)).astype(out_refs[k].dtype)


def line_sum_kernel(*refs):
    xs, ys, out_ref = refs[:LINE], refs[LINE : 2 * LINE], refs[2 * LINE]
    for at, parts in ((0, xs), (BLOCK, ys)):
        out_ref[:, at : at + BLOCK] = sum(p[...].astype(F32) for p in parts).astype(BF16)


def output_kernel(in_ref, wq_ref, wk_ref, wv_ref, wo_ref, out_ref, grad_ref):
    gk = jnp.concatenate([in_ref[h, :BLOCK, :HEAD_DIM] for h in range(HEADS)], axis=1)
    gv = jnp.concatenate([in_ref[h, :BLOCK, HEAD_DIM:] for h in range(HEADS)], axis=1)
    gq = jnp.concatenate([in_ref[h, BLOCK : BLOCK + HEAD_DIM] for h in range(HEADS)], axis=0)
    att = jnp.concatenate([in_ref[h, BLOCK + HEAD_DIM :] for h in range(HEADS)], axis=0)
    out = lax.dot_general(att, wo_ref[...], TN, preferred_element_type=F32)
    out_ref[...] = out.astype(BF16)
    total = lax.dot_general(
        gq, wq_ref[...], (((0,), (1,)), ((), ())), preferred_element_type=F32
    )
    total = total + lax.dot_general(gk, wk_ref[...], NT, preferred_element_type=F32)
    total = total + lax.dot_general(gv, wv_ref[...], NT, preferred_element_type=F32)
    grad_ref[...] = total.astype(BF16)


def ctx_shift(x, dy=0, dx=0, dc=0):
    pairs = []
    for i in range(LINE * LINE * CORES):
        y, r, c = i // (LINE * CORES), i // CORES % LINE, i % CORES
        to = ((y + dy) % LINE * LINE + (r + dx) % LINE) * CORES + (c + dc) % CORES
        pairs.append((i, to))
    return lax.ppermute(x, "ctx", pairs)


def live_lists(block_cell, cell_mask, y, xc):
    cells = jnp.arange(cell_mask.shape[0], dtype=jnp.int32)
    by_line = block_cell.reshape(LINE, LINE * CORES, OWN)
    q_cell = lax.dynamic_index_in_dim(by_line, xc, 1, keepdims=False).reshape(Q_BLOCKS)
    k_cell = lax.dynamic_slice_in_dim(block_cell, y * K_BLOCKS, K_BLOCKS, 0)
    q_hot = (q_cell[:, None] == cells[None, :]).astype(BF16)
    k_hot = (k_cell[:, None] == cells[None, :]).astype(BF16)
    picked = jnp.dot(q_hot, cell_mask.astype(BF16), preferred_element_type=F32).astype(BF16)
    live = lax.dot_general(picked, k_hot, NT, preferred_element_type=F32)
    at = jnp.arange(K_BLOCKS, dtype=jnp.int32)
    upto = (at[:, None] <= at[None, :]).astype(BF16)
    rank = jnp.dot(live.astype(BF16), upto, preferred_element_type=F32)
    slots = jnp.arange(1, SLOTS + 1, dtype=jnp.int32).astype(F32)
    matched = (live[:, None, :] > 0.5) & (rank[:, None, :] == slots[None, :, None])
    pos = jnp.sum(jnp.where(matched, at[None, None, :], 0), axis=2)
    return pos, jnp.sum(live, axis=1).astype(jnp.int32)


def item_table(amounts, first, most):
    b = jnp.arange(Q_BLOCKS, dtype=jnp.int32)
    j = jnp.arange(most, dtype=jnp.int32)
    start = jnp.sum(jnp.where(b[None, :] < b[:, None], amounts[None, :], 0), axis=1)
    at = jnp.where(j[None, :] < amounts[:, None], start[:, None] + j[None, :], -1)
    code = (b * 16 + first)[:, None] + j[None, :]
    slot = jnp.arange(Q_BLOCKS * most, dtype=jnp.int32)
    hit = at[None] == slot[:, None, None]
    return jnp.sum(jnp.where(hit, code[None], 0), axis=(1, 2)), jnp.sum(amounts)[None]


def item_tables(cnt):
    half = GRADS_ITEM // 2
    none = jnp.zeros_like(cnt)
    whole = (cnt + half - 1) // GRADS_ITEM
    left = cnt % GRADS_ITEM
    short = ((left > 0) & (left <= half)).astype(jnp.int32)
    stats = item_table((cnt + STATS_ITEM - 1) // STATS_ITEM, none, STATS_MOST)
    wholes = item_table(whole, none, GRADS_MOST)
    halves = item_table(short, 2 * whole, 1)
    return jnp.concatenate(stats), jnp.concatenate(wholes + halves)


def exchange(x):
    return lax.all_to_all(x, "head", split_axis=0, concat_axis=0, tiled=True)


LINES = (struct((K_BLOCKS * BLOCK, WIDE), BF16), struct((Q_BLOCKS * BLOCK, WIDE), BF16))


def piece_sems():
    return pltpu.SemaphoreType.DMA((3 * LINE,))


MIXED = [struct((OWN, BLOCK, WIDE), F32)] + [struct((OWN, BLOCK, WIDE), BF16)] * (LINE - 1)


def stats_call(lists, kvs, qds):
    return call(
        stats_kernel,
        (struct((3, Q_BLOCKS, BLOCK), F32),) + LINES,
        [SMEM] * 4 + [VMEM] * (3 * LINE),
        [piece_sems()],
        "stats",
    )(*lists, *near(*kvs, *qds))


def grads_call(lists, stats, kv, qd):
    return call(
        grads_kernel,
        MIXED + [struct((LINE * OWN, BLOCK, WIDE), F32), struct((LINE * OWN, BLOCK, WIDE), BF16)],
        [SMEM] * 4 + [VMEM] * (LINE + 2),
        [pltpu.VMEM((K_BLOCKS, BLOCK, WIDE), F32), pltpu.VMEM((Q_BLOCKS, BLOCK, WIDE), F32)]
        + [pltpu.VMEM((Q_BLOCKS, BLOCK), F32)] * 2,
        "grads",
    )(*lists, *near(*stats, kv, qd))


def body(hits_in, w_query, w_key, w_value, w_out, grad_y, block_cell, cell_mask):
    rows = OWN * BLOCK
    ctx = lax.axis_index("ctx")
    y, x, core = ctx // (LINE * CORES), ctx // CORES % LINE, ctx % CORES
    me = jnp.stack([y, x, core]).astype(jnp.int32)
    pos, cnt = live_lists(block_cell, cell_mask, y, ctx % (LINE * CORES))

    wide = (HEADS, 2 * BLOCK, WIDE)
    given = (hits_in, w_key, w_value, w_query, grad_y, w_out)
    sent = call(
        project_kernel,
        struct(wide, BF16),
        [ANY] * 6,
        [pltpu.VMEM(g.shape, BF16) for g in given] + [pltpu.SemaphoreType.DMA((6,))],
        "project",
    )(*[pltpu.with_memory_space_constraint(g, pltpu.HBM) for g in given])
    tables = item_tables(cnt)
    got, me, pos, cnt, tables = lax.optimization_barrier((exchange(sent), me, pos, cnt, tables))
    kv = got[:, :BLOCK].reshape(rows, WIDE)
    qd = got[:, BLOCK:].reshape(rows, WIDE)
    kvs = [kv] + [ctx_shift(kv, dx=hop) for hop in HOPS[1:]]
    other = ctx_shift(kv, dc=1)
    qd, other = lax.optimization_barrier((qd, other))
    kvs = kvs + [other] + [ctx_shift(piece, dc=1) for piece in kvs[1:]]
    qds = [qd] + [ctx_shift(qd, dy=hop) for hop in HOPS[1:]]

    stats, kv_lines, qd_lines = stats_call((me, pos, cnt, tables[0]), kvs, qds)
    all_stats = [stats] + [ctx_shift(stats, dy=hop) for hop in HOPS[1:]]
    *y_parts, own, other = grads_call(
        (me, pos, cnt, tables[1]), all_stats, kv_lines, qd_lines
    )
    other = ctx_shift(other, dc=1)
    x_parts = call(core_sum_kernel, MIXED, [SMEM, VMEM, VMEM], name="core_sum")(
        me, *near(own, other)
    )
    x_parts = list(x_parts)
    y_parts[3], x_parts[3] = lax.optimization_barrier((y_parts[3], x_parts[3]))
    y_parts = [y_parts[0]] + [ctx_shift(p, dy=hop) for p, hop in zip(y_parts[1:], HOPS[1:])]
    x_parts = [x_parts[0]] + [ctx_shift(p, dx=hop) for p, hop in zip(x_parts[1:], HOPS[1:])]
    summed = call(line_sum_kernel, struct(wide, BF16), [VMEM] * (2 * LINE), name="line_sum")(
        *near(*x_parts, *y_parts)
    )
    full = struct(hits_in.shape, BF16)
    return call(output_kernel, (full, full), [VMEM] * 5, name="output")(
        *near(exchange(summed), w_query, w_key, w_value, w_out)
    )


def solution(mesh):
    row = P(("ctx", "head"), None)
    return jax.shard_map(
        body,
        mesh=mesh,
        in_specs=(row, P(), P(), P(), P(), row, P(), P()),
        out_specs=(row, row),
        check_vma=False,
    )
```
